256 devices in a mesh: pipe: 8 (over z_lo, core), expert: 32 (over x, y, z_hi).
Axes of the slice: x: 4, y: 4, z: 8 (z_hi: 2, z_lo: 4; z = z_hi * 4 + z_lo), core: 2. Of those that a mesh axis runs over, the one named last changes fastest.
Arguments:
- a_input: bfloat16 [8, 4096, 3584], P('pipe', 'expert'), may hold values from -6 to 6
- a_route: int32 [8, 4096, 1], P('pipe', 'expert'), may hold values from 0 to 7; in each aligned block of 128 rows (0 to 127, 128 to 255, ..., all dimensions but the last counted through in order) at most 18 rows name the same one
- b_saved: bfloat16 [8, 4096, 3584], P('pipe', 'expert'), may hold values from -6 to 6
- b_grad: bfloat16 [8, 4096, 3584], P('pipe', 'expert'), may hold values from -6 to 6
- b_route: int32 [8, 4096, 1], P('pipe', 'expert'), may hold values from 0 to 7; in each aligned block of 128 rows (0 to 127, 128 to 255, ..., all dimensions but the last counted through in order) at most 18 rows name the same one
- up_weight: bfloat16 [8, 3584, 8192], P('pipe', None, 'expert'), may hold values from -0.09375 to 0.09375
- down_weight: bfloat16 [8, 8192, 3584], P('pipe', 'expert'), may hold values from -0.1875 to 0.1875
- router: bfloat16 [8, 3584, 8], P('pipe'), may hold values from -0.09375 to 0.09375
Outputs:
- a_next: bfloat16 [8, 4096, 3584], P('pipe', 'expert')
- b_next: bfloat16 [8, 4096, 3584], P('pipe', 'expert')
- up_grad: bfloat16 [8, 3584, 8192], P('pipe', None, 'expert')
- down_grad: bfloat16 [8, 8192, 3584], P('pipe', 'expert')
The draws below stay inside these ranges and needn't reach their ends.
Inputs may be any that keep to these rules, and one draw needn't show every extreme that they name: `a_route`: within each device's 128 rows, no expert is named by more than 18 of the (token, choice) pairs, a bound that some block reaches. `b_route`: within each device's 128 rows, no expert is named by more than 18 of the (token, choice) pairs, a bound that some block reaches.
All inputs are finite; a program needn't handle non-finite values.
Results may differ from the reference program's by a relative error of at most 0.0067.
Values may be sent and summed in bfloat16 or wider, within the bound.
A program may use at most 128 MiB of HBM per device.

```python
import math
import jax
import jax.numpy as jnp
import numpy as np
from jax import lax

D = 3584
FF = 1024
GROUP = 4
TOP = 1
TOK = 128
HID = 256
EXPERTS = 8
CAP = 18
TOKENS = 4096
N_PIPE = 8
N_EXPERT = 32


def level_of(key, dims, split, smallest, high):
    def one(axis_at, shards_of):
        heights = jax.random.uniform(jax.random.fold_in(jax.random.fold_in(key, 6), axis_at), (shards_of,), jnp.float32, smallest / len(split), high / len(split))
        return jnp.repeat(jnp.exp(heights), dims[axis_at] // shards_of).reshape((-1,) + (1,) * (len(dims) - axis_at - 1))

    level = one(*split[0])
    for cut in split[1:]:
        level = level * one(*cut)
    return level


def routed_block(own_key, own, number, rows, amount, top, most, skew):
    ranking = jax.random.permutation(own_key, amount)
    heavy_load, usual = load_shares(amount, rows * top, most, skew, True), load_shares(amount, rows * top, most, skew, False)
    places = jnp.arange(amount)

    def named(sizes, rotation):
        used = int((sizes > 0).sum())
        fixed = max(1, used // 4)
        moved = fixed + (places - fixed + rotation * (used - fixed)) % max(1, amount - fixed)
        return jnp.zeros((amount,), jnp.int32).at[ranking[jnp.where(places < fixed, places, moved)]].set(jnp.asarray(sizes, jnp.int32))

    sizes = jnp.where(number % 4 == 0, named(heavy_load, number // 4), named(usual, number - number // 4 - 1))
    mixed = jax.random.permutation(jax.random.fold_in(own, 3), amount)
    giver, receiver = mixed[0:amount // 2 * 2:2], mixed[1:amount // 2 * 2:2]
    margin = jnp.minimum(sizes[giver] - 1, most - sizes[receiver]) // 2
    margin = jnp.where((giver == ranking[0]) | (receiver == ranking[0]) | (sizes[receiver] == 0), 0, jnp.maximum(margin, 0))
    moved = jax.random.randint(jax.random.fold_in(own, 4), (amount // 2,), 0, 1 << 20) % (margin + 1)
    sizes = sizes.at[giver].add(-moved).at[receiver].add(moved)
    labels = jnp.searchsorted(jnp.cumsum(sizes), jnp.arange(rows * top), side="right").astype(jnp.int32)
    grid = labels.reshape(top, rows).T
    grid = grid[jax.random.permutation(jax.random.fold_in(own, 1), rows)]
    rotation = jax.random.randint(jax.random.fold_in(own, 2), (rows, 1), 0, top)
    return jnp.take_along_axis(grid, (jnp.arange(top)[None, :] + rotation) % top, axis=1)


def load_shares(number_of, total, bound, slope, full):
    loads = [(1 << 20) // math.isqrt(grade ** slope) + 1 for grade in range(1, number_of + 1)]
    largest = bound if full else min(bound, max(-(-total // number_of), total * loads[0] // sum(loads)))
    least = 1 if total - largest >= number_of - 1 else 0
    counts, rest = [largest] + [least] * (number_of - 1), total - largest - least * (number_of - 1)
    while rest > 0:
        movable = [i for i in range(1, number_of) if counts[i] < largest] or [i for i in range(1, number_of) if counts[i] < bound]
        mass, budget = sum([loads[i] for i in movable]), rest
        for i in movable:
            more = min(bound - counts[i], max(1, budget * loads[i] // mass), rest)
            counts[i] = counts[i] + more
            rest = rest - more
    return np.array(counts)


def bell_draw(rng, shape, scale, limit, pieces=(), kind=jnp.bfloat16):
    level = level_of(rng, shape, pieces, -0.22, 0.18) if pieces else 1.0
    result = jax.random.normal(rng, shape, jnp.float32) * scale * level
    return jnp.minimum(jnp.maximum(result, -limit), limit).astype(kind)


def setup_inputs(seed: int = 0) -> dict:
    keys = jax.random.split(jax.random.key(seed), 9)
    a_input = bell_draw(keys[0], (N_PIPE, TOKENS, D), 1.0, 6.0, ((0, 8), (1, 32)))
    a_route_keys = jax.random.split(jax.random.fold_in(keys[1], 1), N_PIPE * TOKENS // TOK)
    a_route_turns = jax.random.permutation(jax.random.fold_in(keys[1], 3), N_PIPE * TOKENS // TOK)
    a_route = jax.vmap(lambda own, number: routed_block(jax.random.fold_in(keys[1], 2), own, number, TOK, EXPERTS, TOP, CAP, 1))(a_route_keys, a_route_turns).reshape((N_PIPE, TOKENS, TOP))
    b_saved = bell_draw(keys[2], (N_PIPE, TOKENS, D), 1.0, 6.0, ((0, 8), (1, 32)))
    b_grad = bell_draw(keys[3], (N_PIPE, TOKENS, D), 1.0, 6.0, ((0, 8), (1, 32)))
    b_route_keys = jax.random.split(jax.random.fold_in(keys[4], 1), N_PIPE * TOKENS // TOK)
    b_route_turns = jax.random.permutation(jax.random.fold_in(keys[4], 3), N_PIPE * TOKENS // TOK)
    b_route = jax.vmap(lambda own, number: routed_block(jax.random.fold_in(keys[4], 2), own, number, TOK, EXPERTS, TOP, CAP, 1))(b_route_keys, b_route_turns).reshape((N_PIPE, TOKENS, TOP))
    up_weight = bell_draw(keys[5], (N_PIPE, D, EXPERTS * FF), D ** -0.5, 0.09375, ((0, 8), (2, 32)))
    down_weight = bell_draw(keys[6], (N_PIPE, EXPERTS * FF, D), FF ** -0.5, 0.1875, ((0, 8), (1, 32)))
    router = bell_draw(keys[7], (N_PIPE, D, EXPERTS), D ** -0.5, 0.09375, ((0, 8),))
    return dict(a_input=a_input, a_route=a_route, b_saved=b_saved, b_grad=b_grad, b_route=b_route, up_weight=up_weight, down_weight=down_weight, router=router)


EPS = 1e-06

def rounded(values):
    return lax.optimization_barrier(values.astype(jnp.bfloat16)).astype(jnp.float32)

def positions(route_ids):
    blocks = route_ids.reshape(N_EXPERT, TOK * TOP).astype(jnp.int32)
    onehot = (blocks[:, :, None] == jnp.arange(EXPERTS, dtype=jnp.int32)).astype(jnp.int32)
    slot_pos = lax.optimization_barrier(jnp.sum(onehot * (jnp.cumsum(onehot, axis=1) - 1), axis=2)).astype(jnp.int32)
    source = jnp.arange(N_EXPERT, dtype=jnp.int32)[:, None]
    return (blocks * (N_EXPERT * CAP) + source * CAP + slot_pos).reshape(-1).astype(jnp.int32)

def plan(features, route_ids, router_cols):
    feat_float = features.astype(jnp.float32)
    inv_scale = lax.rsqrt(lax.optimization_barrier(jnp.mean(feat_float * feat_float, axis=-1, keepdims=True)) + EPS)
    normed = (feat_float * inv_scale).astype(jnp.bfloat16)
    scores = jnp.dot(normed, router_cols, preferred_element_type=jnp.float32)
    gate_value = jax.nn.sigmoid(jnp.take_along_axis(scores, route_ids, axis=1))
    return (feat_float, inv_scale, normed, gate_value, positions(route_ids))

def spread(row_block, flat_index):
    buffer = jnp.zeros((EXPERTS * N_EXPERT * CAP, D), row_block.dtype).at[flat_index].set(row_block)
    return buffer.reshape(EXPERTS, N_EXPERT * CAP, D)

def section_weights(up_section, down_section):
    return (up_section.reshape(D, EXPERTS, FF).transpose(1, 0, 2), down_section.reshape(EXPERTS, FF, D))

def expert_forward(row_block, up_expert, down_expert):
    hidden = jnp.dot(row_block, up_expert, preferred_element_type=jnp.float32)
    sigma_vals = jax.nn.sigmoid(hidden)
    activated = (hidden * sigma_vals).astype(jnp.bfloat16)
    partial_value = jnp.einsum('rgh,ghd->grd', activated.reshape(-1, GROUP, HID).astype(jnp.float32), down_expert.reshape(GROUP, HID, D).astype(jnp.float32))
    return (hidden, sigma_vals, activated, partial_value.astype(jnp.bfloat16))

def forward_section(features, route_ids, up_section, down_section, router_cols):
    feat_float, inv_scale, normed, gate_value, flat_index = plan(features, route_ids, router_cols)
    buffers = spread(jnp.repeat(normed, TOP, axis=0), flat_index)
    ups, downs = section_weights(up_section, down_section)

    def one_expert(operands):
        partial_value = expert_forward(operands[0], operands[1], operands[2])[3]
        return lax.optimization_barrier(jnp.sum(partial_value.astype(jnp.float32), axis=0))
    expert_out = rounded(lax.map(one_expert, (buffers, ups, downs))).reshape(-1, D)
    token_out = expert_out[flat_index].reshape(TOKENS, TOP, D)
    return (feat_float + lax.optimization_barrier(jnp.sum(gate_value[:, :, None] * token_out, axis=1))).astype(jnp.bfloat16)

def backward_section(features, cotangent, route_ids, up_section, down_section, router_cols):
    feat_float, inv_scale, normed, gate_value, flat_index = plan(features, route_ids, router_cols)
    buffers = spread(jnp.repeat(normed, TOP, axis=0), flat_index)
    cot_rows = (gate_value[:, :, None] * cotangent.astype(jnp.float32)[:, None, :]).astype(jnp.bfloat16).reshape(-1, D)
    cot_buffers = spread(cot_rows, flat_index)
    ups, downs = section_weights(up_section, down_section)

    def one_expert(operands):
        row_block, cot_block, up_expert, down_expert = operands
        hidden, sigma_vals, activated, partial_value = expert_forward(row_block, up_expert, down_expert)
        gate_term = rounded(lax.optimization_barrier(jnp.sum(rounded(lax.optimization_barrier(jnp.sum(cot_block.astype(jnp.float32)[None] * partial_value.astype(jnp.float32), axis=2))), axis=0)))
        act_grad = jnp.dot(cot_block, down_expert.T, preferred_element_type=jnp.float32)
        hid_grad = (act_grad * sigma_vals * (1.0 + hidden * (1.0 - sigma_vals))).astype(jnp.bfloat16)
        grad_down = jnp.dot(activated.T, cot_block, preferred_element_type=jnp.float32).astype(jnp.bfloat16)
        grad_up = jnp.dot(row_block.T, hid_grad, preferred_element_type=jnp.float32).astype(jnp.bfloat16)
        up_groups = up_expert.reshape(D, GROUP, HID).transpose(1, 2, 0).astype(jnp.float32)
        input_part = jnp.einsum('rgh,ghd->grd', hid_grad.reshape(-1, GROUP, HID).astype(jnp.float32), up_groups)
        input_sum = rounded(lax.optimization_barrier(jnp.sum(rounded(input_part), axis=0)))
        return (grad_up, grad_down, input_sum, gate_term)
    grad_ups, grad_downs, input_sums, gate_terms = lax.map(one_expert, (buffers, cot_buffers, ups, downs))
    input_tok = lax.optimization_barrier(jnp.sum(input_sums.reshape(-1, D)[flat_index].reshape(TOKENS, TOP, D), axis=1))
    score_grad = gate_terms.reshape(-1)[flat_index].reshape(TOKENS, TOP) * (1.0 - gate_value)
    onehot = (route_ids[:, :, None] == jnp.arange(EXPERTS, dtype=jnp.int32)).astype(jnp.float32)
    full_grad = lax.optimization_barrier(jnp.sum(onehot * score_grad[:, :, None], axis=1))
    normed_grad = input_tok + jnp.dot(full_grad, router_cols.astype(jnp.float32).T, precision=lax.Precision.HIGHEST)
    cubed = inv_scale * inv_scale * inv_scale
    feature_grad = inv_scale * normed_grad - feat_float * cubed * lax.optimization_barrier(jnp.sum(normed_grad * feat_float, axis=-1, keepdims=True)) / D
    input_grad = (cotangent.astype(jnp.float32) + feature_grad).astype(jnp.bfloat16)
    up_full = grad_ups.transpose(1, 0, 2).reshape(D, EXPERTS * FF)
    down_full = grad_downs.reshape(EXPERTS * FF, D)
    return (input_grad, up_full, down_full)

def reference(a_input, a_route, b_saved, b_grad, b_route, up_weight, down_weight, router):
    a_outs = []
    b_outs = []
    up_grads = []
    down_grads = []
    for section_index in range(N_PIPE):
        a_outs.append(forward_section(a_input[section_index], a_route[section_index], up_weight[section_index], down_weight[section_index], router[section_index]))
        source = N_PIPE - 1 - section_index
        input_grad, up_full, down_full = backward_section(b_saved[source], b_grad[source], b_route[source], up_weight[section_index], down_weight[section_index], router[section_index])
        b_outs.append(input_grad)
        up_grads.append(up_full)
        down_grads.append(down_full)
    a_next = jnp.stack([a_outs[(j - 1) % N_PIPE] for j in range(N_PIPE)])
    b_next = jnp.stack([b_outs[(N_PIPE - j) % N_PIPE] for j in range(N_PIPE)])
    return (a_next, b_next, jnp.stack(up_grads), jnp.stack(down_grads))
```

```python
import jax
import jax.numpy as jnp
from jax import lax
from jax.experimental import pallas as pl
from jax.experimental.pallas import tpu as pltpu
from jax.sharding import PartitionSpec as P

EPS = 1e-06
MESH = pl.DeviceIdType.MESH
TOK = 128
D = 3584
CAP = 18
EXPERTS = 8
SIDE = 4
PLANE = 16
PARTS = 4
W = D // PARTS
WIDE = 9 * W
BF = jnp.bfloat16
NEAR = sorted(
    [(i, j) for i in range(SIDE) for j in range(SIDE) if i or j],
    key=lambda s: min(s[0], SIDE - s[0]) + min(s[1], SIDE - s[1]),
)


class Place:
    def __init__(self):
        self.pipe = lax.axis_index("pipe")
        self.expert = lax.axis_index("expert")
        self.half = lax.rem(self.expert, 2)
        self.spot = self.expert // 2
        self.x = self.spot // SIDE
        self.y = lax.rem(self.spot, SIDE)
        self.across = self.expert + 1 - 2 * self.half

    def spot_at(self, dx, dy):
        return lax.rem(self.x + dx, SIDE) * SIDE + lax.rem(self.y + dy, SIDE)

    def plane(self, spot):
        return (self.pipe, spot * 2 + self.half)


def remote(src, dst, send, recv, device):
    return pltpu.make_async_remote_copy(
        src_ref=src, dst_ref=dst, send_sem=send, recv_sem=recv, device_id=device, device_id_type=MESH
    )


def cols(at, width=W):
    return pl.ds(pl.multiple_of(at * W, 128), width)


def rows16(e):
    return pl.ds(pl.multiple_of(e * 16, 16), 16)


def selector(kind, code, part=0):
    row = lax.broadcasted_iota(jnp.int32, (TOK, TOK), 0)
    e, slot = code // 32, code % 32
    if kind == "own0":
        to, ok = slot, slot < 16
    elif kind == "own1":
        to, ok = slot - 16, slot >= 16
    elif kind == "far1":
        to, ok = slot + 2, slot < 14
    else:
        to, ok = slot - 14 + 4 * part, slot >= 14
    return ((row == e * 16 + to) & ok).astype(jnp.float32).astype(BF)


def fill_selectors(sel, t, own_code, far_code):
    sel[t, 0] = selector("own0", own_code)
    sel[t, 1] = selector("own1", own_code)
    sel[t, 2] = selector("far1", far_code)
    for q in range(PARTS):
        sel[t, 3 + q] = selector("left", far_code, q)


def dot(a, b):
    return jnp.dot(a, b, preferred_element_type=jnp.float32)


def dispatch_kernel(
    ax, bx, bc, acode, bcode, ra, rbx, rbc, bc_own, far_codes,
    own_a, far_a, got_b, codes, send_a, send_bx, send_bc, left, sel,
    zsend, zrecv, csend, crecv, psend, precv, local,
):
    me = Place()
    across = (me.pipe, me.across)
    mirror = (7 - me.pipe, me.expert)
    mirror_across = (7 - me.pipe, me.across)
    barrier = pltpu.get_barrier_semaphore()
    greet = [me.plane(me.spot_at(i, j)) for i, j in NEAR] + [across, mirror, mirror_across]
    for device in greet:
        pl.semaphore_signal(barrier, inc=1, device_id=device, device_id_type=MESH)
    load = pltpu.make_async_copy(ax, own_a, local.at[0])
    load.start()
    pl.semaphore_wait(barrier, len(greet))

    small = [
        remote(acode, codes.at[0], csend.at[0], crecv.at[0], across),
        remote(bcode, codes.at[1], csend.at[1], crecv.at[1], mirror),
        remote(bcode, codes.at[2], csend.at[2], crecv.at[2], mirror_across),
    ]
    for copy in small:
        copy.start()

    def z_copy(lane, q):
        src, dst, to = [
            (ax, far_a, across),
            (bx, got_b.at[0], mirror),
            (bx, got_b.at[1], mirror_across),
            (bc, got_b.at[2], mirror),
            (bc, got_b.at[3], mirror_across),
        ][lane]
        return remote(src.at[:, cols(q)], dst.at[:, cols(q)], zsend.at[lane, q], zrecv.at[lane, q], to)

    for lanes in ((0,), (1, 2), (3, 4)):
        @pl.loop(0, PARTS)
        def _(q):
            for lane in lanes:
                z_copy(lane, q).start()

    def spread(t, send, recv, at):
        pltpu.make_async_copy(
            send.at[rows16(me.spot // 2), cols(at)], recv.at[me.spot, :, cols(at)], precv.at[t]
        ).start()
        for i, j in NEAR:
            to = me.spot_at(i, j)
            remote(
                send.at[rows16(to // 2), cols(at)], recv.at[me.spot, :, cols(at)],
                psend.at[t], precv.at[t], me.plane(to),
            ).start()

    load.wait()
    sel[0, 0] = selector("own0", acode[0:1, :])

    @pl.loop(0, PARTS)
    def _(q):
        send_a[:, cols(q)] = dot(sel[0, 0], own_a[:, cols(q)]).astype(BF)
        spread(0, send_a, ra, q)

    small[0].wait()
    fill_selectors(sel, 0, acode[0:1, :], codes[0, 0:1, :])
    left[...] = jnp.zeros_like(left)

    @pl.loop(0, PARTS)
    def _(q):
        z_copy(0, q).wait()
        far = far_a[:, cols(q)]
        send_a[:, cols(PARTS + q)] = (dot(sel[0, 1], own_a[:, cols(q)]) + dot(sel[0, 2], far)).astype(BF)
        left[...] += dot(sel[0, 3 + q], far)
        spread(0, send_a, ra, PARTS + q)

    send_a[:, 2 * D:] = left[...].astype(BF)
    spread(0, send_a, ra, 2 * PARTS)

    small[1].wait()
    small[2].wait()
    fill_selectors(sel, 1, codes[1, 0:1, :], codes[2, 0:1, :])
    for t, send, recv in ((1, send_bx, rbx), (2, send_bc, rbc)):
        near_at, far_at = 2 * t - 2, 2 * t - 1
        left[...] = jnp.zeros_like(left)

        @pl.loop(0, PARTS)
        def _(q):
            z_copy(2 * t - 1, q).wait()
            own = got_b[near_at, :, cols(q)]
            send[:, cols(q)] = dot(sel[1, 0], own).astype(BF)
            spread(t, send, recv, q)
            z_copy(2 * t, q).wait()
            far = got_b[far_at, :, cols(q)]
            send[:, cols(PARTS + q)] = (dot(sel[1, 1], own) + dot(sel[1, 2], far)).astype(BF)
            left[...] += dot(sel[1, 3 + q], far)
            spread(t, send, recv, PARTS + q)

        send[:, 2 * D:] = left[...].astype(BF)
        spread(t, send, recv, 2 * PARTS)

    out_c = pltpu.make_async_copy(got_b.at[2], bc_own, local.at[1])
    out_c.start()
    out_codes = pltpu.make_async_copy(codes, far_codes, local.at[2])
    out_codes.start()
    for t, recv in ((0, ra), (1, rbx), (2, rbc)):
        most = recv.at[pl.ds(0, PLANE - 1)]
        remote(most, most, psend.at[t], precv.at[t], across).wait_send()
        pltpu.make_async_copy(recv, recv, precv.at[t]).wait()
    out_c.wait()
    out_codes.wait()


def dispatch(ax, bx, bc, acode, bcode):
    block = jax.ShapeDtypeStruct((PLANE, 16, WIDE), BF)
    anywhere = pl.BlockSpec(memory_space=pl.ANY)
    inside = pl.BlockSpec(memory_space=pltpu.VMEM)
    dma = pltpu.SemaphoreType.DMA
    return pl.pallas_call(
        dispatch_kernel,
        name="dispatch",
        out_shape=(block, block, block, jax.ShapeDtypeStruct((TOK, D), BF),
                   jax.ShapeDtypeStruct((3, 8, TOK), jnp.int32)),
        in_specs=[anywhere] * 3 + [inside] * 2,
        out_specs=(anywhere,) * 5,
        scratch_shapes=[
            pltpu.VMEM((TOK, D), BF), pltpu.VMEM((TOK, D), BF), pltpu.VMEM((4, TOK, D), BF),
            pltpu.VMEM((3, 8, TOK), jnp.int32),
            pltpu.VMEM((TOK, WIDE), BF), pltpu.VMEM((TOK, WIDE), BF), pltpu.VMEM((TOK, WIDE), BF),
            pltpu.VMEM((TOK, W), jnp.float32), pltpu.VMEM((2, 3 + PARTS, TOK, TOK), BF),
            dma((5, PARTS)), dma((5, PARTS)), dma((3,)), dma((3,)), dma((3,)), dma((3,)), dma((3,)),
        ],
        compiler_params=pltpu.CompilerParams(collective_id=1, has_side_effects=True, vmem_limit_bytes=40 << 20),
    )(ax, bx, bc, acode, bcode)


def collect_kernel(
    sa, sb, xa, cb, ua, ub, oa, ob,
    ga, gb, base, own, far, psend, precv, zsend, zrecv, local,
):
    me = Place()
    a_to = lax.rem(me.pipe + 1, 8)
    a_from = lax.rem(me.pipe + 7, 8)
    b_to = lax.rem(8 - me.pipe, 8)
    stays = b_to == me.pipe
    barrier = pltpu.get_barrier_semaphore()
    greet = [me.plane(me.spot_at(i, j)) for i, j in NEAR]
    greet += [(a_to, me.expert), (a_to, me.across), (a_from, me.expert), (a_from, me.across), (b_to, me.across)]
    for device in greet:
        pl.semaphore_signal(barrier, inc=1, device_id=device, device_id_type=MESH)

    @pl.when(jnp.logical_not(stays))
    def _():
        pl.semaphore_signal(barrier, inc=1, device_id=(b_to, me.expert), device_id_type=MESH)

    loads = [
        pltpu.make_async_copy(xa, base.at[0], local.at[0]),
        pltpu.make_async_copy(cb, base.at[1], local.at[1]),
    ]
    for copy in loads:
        copy.start()
    pl.semaphore_wait(barrier, len(greet) + 1 - stays.astype(jnp.int32))

    def spread(t, send, recv, at, sem):
        pltpu.make_async_copy(
            send.at[me.spot, :, cols(at)], recv.at[me.spot, :, cols(at)], precv.at[t, sem]
        ).start()
        for i, j in NEAR:
            to = me.spot_at(i, j)
            remote(
                send.at[to, :, cols(at)], recv.at[me.spot, :, cols(at)],
                psend.at[t], precv.at[t, sem], me.plane(to),
            ).start()

    tensors = ((0, sa, ga, ua, oa, a_to), (1, sb, gb, ub, ob, b_to))
    for t, send, recv, u, out, to in tensors:
        spread(t, send, recv, 2 * PARTS, PARTS)

        @pl.loop(0, PARTS)
        def _(q):
            spread(t, send, recv, PARTS + q, q)
            spread(t, send, recv, q, q)

    for copy in loads:
        copy.wait()

    def flat(ref, at):
        return ref[:, :, cols(at)].reshape(PLANE * 16, W)

    for t, send, recv, u, out, to in tensors:
        edge = recv.at[:, :, pl.ds(2 * D, W)]
        pltpu.make_async_copy(edge, edge, precv.at[t, PARTS]).wait()

        @pl.loop(0, PARTS)
        def _(q):
            both = recv.at[:, :, pl.ds(0, 2 * W)]
            pltpu.make_async_copy(both, both, precv.at[t, q]).wait()
            second = flat(recv, PARTS + q)
            far[t, :, cols(q)] = (dot(u[2], second) + dot(u[3 + q], flat(recv, 2 * PARTS))).astype(BF)
            remote(
                far.at[t, :, cols(q)], out.at[1, :, cols(q)],
                zsend.at[t, 1, q], zrecv.at[t, 1, q], (to, me.across),
            ).start()
            own[t, :, cols(q)] = (
                base[t, :, cols(q)].astype(jnp.float32) + dot(u[0], flat(recv, q)) + dot(u[1], second)
            ).astype(BF)
            send_own = remote(
                own.at[t, :, cols(q)], out.at[0, :, cols(q)],
                zsend.at[t, 0, q], zrecv.at[t, 0, q], (to, me.expert),
            )
            if t == 0:
                send_own.start()
            else:
                @pl.when(stays)
                def _():
                    pltpu.make_async_copy(
                        own.at[t, :, cols(q)], out.at[0, :, cols(q)], zrecv.at[t, 0, q]
                    ).start()

                @pl.when(jnp.logical_not(stays))
                def _():
                    send_own.start()

    for t, send, recv, u, out, to in tensors:
        most = recv.at[pl.ds(0, PLANE - 1)]
        remote(most, most, psend.at[t], precv.at[t, 0], (to, me.across)).wait_send()

        @pl.loop(0, PARTS)
        def _(q):
            remote(
                far.at[t, :, cols(q)], out.at[1, :, cols(q)],
                zsend.at[t, 1, q], zrecv.at[t, 1, q], (to, me.across),
            ).wait()
            if t == 0:
                remote(
                    own.at[t, :, cols(q)], out.at[0, :, cols(q)],
                    zsend.at[t, 0, q], zrecv.at[t, 0, q], (to, me.expert),
                ).wait()
            else:
                @pl.when(jnp.logical_not(stays))
                def _():
                    remote(
                        own.at[t, :, cols(q)], out.at[0, :, cols(q)],
                        zsend.at[t, 0, q], zrecv.at[t, 0, q], (to, me.expert),
                    ).wait()

                @pl.when(stays)
                def _():
                    pltpu.make_async_copy(
                        own.at[t, :, cols(q)], out.at[0, :, cols(q)], zrecv.at[t, 0, q]
                    ).wait()


def collect(sa, sb, xa, cb, ua, ub):
    pair = jax.ShapeDtypeStruct((2, TOK, D), BF)
    anywhere = pl.BlockSpec(memory_space=pl.ANY)
    inside = pl.BlockSpec(memory_space=pltpu.VMEM)
    dma = pltpu.SemaphoreType.DMA
    return pl.pallas_call(
        collect_kernel,
        name="collect",
        out_shape=(pair, pair),
        in_specs=[anywhere] * 4 + [inside] * 2,
        out_specs=(anywhere,) * 2,
        scratch_shapes=[
            pltpu.VMEM((PLANE, 16, WIDE), BF), pltpu.VMEM((PLANE, 16, WIDE), BF),
            pltpu.VMEM((2, TOK, D), BF), pltpu.VMEM((2, TOK, D), BF), pltpu.VMEM((2, TOK, D), BF),
            dma((2,)), dma((2, PARTS + 1)), dma((2, 2, PARTS)), dma((2, 2, PARTS)), dma((2,)),
        ],
        compiler_params=pltpu.CompilerParams(collective_id=2, has_side_effects=True, vmem_limit_bytes=40 << 20),
    )(sa, sb, xa, cb, ua, ub)


def slot_code(route):
    ids = route.reshape(TOK)
    same = ids[:, None] == ids[None, :]
    earlier = jnp.arange(TOK)[:, None] < jnp.arange(TOK)[None, :]
    slot = jnp.sum((same & earlier).astype(jnp.int32), axis=0)
    return jnp.broadcast_to((ids * 32 + slot)[None, :], (8, TOK)).astype(jnp.int32)


def unslot(own_code, far_code):
    lane = jnp.arange(PLANE * 16, dtype=jnp.int32)[None, :]
    e_of, r_of = lane // 32, lane % 16

    def one(code, to, ok):
        return ((code // 32 == e_of) & (r_of == to) & ok).astype(BF)

    own, far = own_code[:, None], far_code[:, None]
    so, sf = own % 32, far % 32
    parts = [one(own, so, so < 16), one(own, so - 16, so >= 16), one(far, sf + 2, sf < 14)]
    parts += [one(far, sf - 14 + 4 * q, sf >= 14) for q in range(PARTS)]
    return jnp.stack(parts)


def to_rows(block):
    flat = block.reshape(PLANE * 16, WIDE)
    tail = flat[:, 2 * D:].reshape(PLANE, PARTS, 4, W).transpose(0, 2, 1, 3).reshape(PLANE * 4, D)
    return jnp.concatenate([flat[:, :D], flat[:, D:2 * D], tail], axis=0)


def from_rows(rows):
    n = PLANE * 16
    tail = rows[2 * n:].reshape(PLANE, 4, PARTS, W).transpose(0, 2, 1, 3).reshape(n, W)
    return jnp.concatenate([rows[:n], rows[n:2 * n], tail], axis=1).reshape(PLANE, 16, WIDE)


def plan(rows, column):
    x = rows.astype(jnp.float32)
    scale = lax.rsqrt(jnp.mean(x * x, axis=1, keepdims=True) + EPS)
    normed = (x * scale).astype(BF)
    score = jnp.sum(normed.astype(jnp.float32) * column[None, :], axis=1, keepdims=True)
    return x, scale, normed, jax.nn.sigmoid(score)


def mm(a, b, ca, cb):
    return lax.dot_general(a, b, (((ca,), (cb,)), ((), ())), preferred_element_type=jnp.float32)


def body(a_input, a_route, b_saved, b_grad, b_route, up_weight, down_weight, router):
    up, down = up_weight[0], down_weight[0]
    group = lax.axis_size("expert") // EXPERTS
    mine = lax.axis_index("expert") // group
    column = lax.dynamic_slice(router[0], (0, mine), (D, 1))[:, 0].astype(jnp.float32)
    a_code, b_code = slot_code(a_route[0]), slot_code(b_route[0])
    ra, rbx, rbc, c_own, codes = dispatch(a_input[0], b_saved[0], b_grad[0], a_code, b_code)
    ua = unslot(a_code[0], codes[0, 0])
    ub = unslot(codes[1, 0], codes[2, 0])

    _, _, normed, gate = plan(to_rows(ra), column)
    hidden = mm(normed, up, 1, 0)
    act = (hidden * jax.nn.sigmoid(hidden)).astype(BF)
    a_ret = from_rows((gate * mm(act, down, 1, 0)).astype(BF))

    x, scale, normed, gate = plan(to_rows(rbx), column)
    cot = (gate * to_rows(rbc).astype(jnp.float32)).astype(BF)
    hidden = mm(normed, up, 1, 0)
    sig = jax.nn.sigmoid(hidden)
    act = (hidden * sig).astype(BF)
    act_grad = mm(cot, down, 1, 1)
    gate_part = jnp.sum(act.astype(jnp.float32) * act_grad, axis=1, keepdims=True)
    hid_grad = (act_grad * sig * (1.0 + hidden * (1.0 - sig))).astype(BF)
    grad = mm(hid_grad, up, 1, 1) + (gate_part * (1.0 - gate)) * column[None, :]
    along = jnp.sum(grad * x, axis=1, keepdims=True)
    b_ret = from_rows((scale * grad - x * (scale * scale * scale) * along / D).astype(BF))

    out_a, out_b = collect(a_ret, b_ret, a_input[0], c_own, ua, ub)
    down_grad = mm(act, cot, 0, 0).astype(BF)
    up_grad = mm(normed, hid_grad, 0, 0).astype(BF)
    a_next = (out_a[0].astype(jnp.float32) + out_a[1].astype(jnp.float32)).astype(BF)
    b_next = (out_b[0].astype(jnp.float32) + out_b[1].astype(jnp.float32)).astype(BF)
    return a_next[None], b_next[None], up_grad[None], down_grad[None]


def solution(mesh):
    rows = P("pipe", "expert", None)
    return jax.shard_map(
        body,
        mesh=mesh,
        in_specs=(rows, rows, rows, rows, rows, P("pipe", None, "expert"), rows, P("pipe", None, None)),
        out_specs=(rows, rows, P("pipe", None, "expert"), rows),
        check_vma=False,
    )
```

```python
import jax
import jax.numpy as jnp
from jax import lax
from jax.experimental import pallas as pl
from jax.experimental.pallas import tpu as pltpu
from jax.sharding import PartitionSpec as P

EPS = 1e-06
MESH = pl.DeviceIdType.MESH
TOK = 128
D = 3584
CAP = 18
EXPERTS = 8
SIDE = 4
PLANE = 16
PARTS = 4
W = D // PARTS
WIDE = 9 * W
HID = 256
TAIL = 4 * PLANE
ROWS = 2 * PLANE * 16 + TAIL
BF = jnp.bfloat16
NEAR = sorted(
    [(i, j) for i in range(SIDE) for j in range(SIDE) if i or j],
    key=lambda s: min(s[0], SIDE - s[0]) + min(s[1], SIDE - s[1]),
)


class Place:
    def __init__(self):
        self.pipe = lax.axis_index("pipe")
        self.expert = lax.axis_index("expert")
        self.half = lax.rem(self.expert, 2)
        self.spot = self.expert // 2
        self.x = self.spot // SIDE
        self.y = lax.rem(self.spot, SIDE)
        self.across = self.expert + 1 - 2 * self.half

    def spot_at(self, dx, dy):
        return lax.rem(self.x + dx, SIDE) * SIDE + lax.rem(self.y + dy, SIDE)

    def plane(self, spot):
        return (self.pipe, spot * 2 + self.half)


def remote(src, dst, send, recv, device):
    return pltpu.make_async_remote_copy(
        src_ref=src, dst_ref=dst, send_sem=send, recv_sem=recv, device_id=device, device_id_type=MESH
    )


def cols(at, width=W):
    return pl.ds(pl.multiple_of(at * W, 128), width)


def part_rows(q):
    return pl.ds(pl.multiple_of(q * W, 128), W)


def rows16(e):
    return pl.ds(pl.multiple_of(e * 16, 16), 16)


def selector(kind, code, part=0):
    row = lax.broadcasted_iota(jnp.int32, (TOK, TOK), 0)
    return ((row == code // 32 * 16 + place(kind, code % 32, part)) & allowed(kind, code % 32)).astype(jnp.float32).astype(BF)


def place(kind, slot, part):
    return {"own0": slot, "own1": slot - 16, "far1": slot + 2, "left": slot - 14 + 4 * part}[kind]


def allowed(kind, slot):
    return {"own0": slot < 16, "own1": slot >= 16, "far1": slot < 14, "left": slot >= 14}[kind]


def unselector(kind, code, part=0):
    lane = lax.broadcasted_iota(jnp.int32, (TOK, PLANE * 16), 1)
    slot = code % 32
    hit = (lane // 32 == code // 32) & (lane % 16 == place(kind, slot, part)) & allowed(kind, slot)
    return hit.astype(jnp.float32).astype(BF)


def fill_selectors(make, sel, t, own_code, far_code):
    sel[t, 0] = make("own0", own_code)
    sel[t, 1] = make("own1", own_code)
    sel[t, 2] = make("far1", far_code)
    for q in range(PARTS):
        sel[t, 3 + q] = make("left", far_code, q)


def dot(a, b):
    return jnp.dot(a, b, preferred_element_type=jnp.float32)


def dot_nt(a, b):
    return lax.dot_general(a, b, (((1,), (1,)), ((), ())), preferred_element_type=jnp.float32)


def dot_tn(a, b):
    return lax.dot_general(a, b, (((0,), (0,)), ((), ())), preferred_element_type=jnp.float32)


def gather_tail(q):
    r = lax.broadcasted_iota(jnp.int32, (TAIL, PLANE * 16), 0)
    c = lax.broadcasted_iota(jnp.int32, (TAIL, PLANE * 16), 1)
    return ((c // 16 == r // 4) & (c % 16 == 4 * q + r % 4)).astype(jnp.float32).astype(BF)


def spread_tail(q):
    c = lax.broadcasted_iota(jnp.int32, (PLANE * 16, TAIL), 0)
    r = lax.broadcasted_iota(jnp.int32, (PLANE * 16, TAIL), 1)
    return ((c // 16 == r // 4) & (c % 16 == 4 * q + r % 4)).astype(jnp.float32).astype(BF)


def span_kernel(
    ax, bx, bc, acode, bcode, acol, bcol, up_in, down_in, column,
    oa, ob, up_out, down_out,
    own_a, far_a, got_b, codes, code_cols, send_a, send_bx, send_bc, ra, rbx, rbc,
    ret_a, ret_b, ga, gb, own, far, up, down, up_grad, down_grad,
    left, sel, sums, tails, tail_ret, hidden, act_grad, act, hid_grad, stat,
    zsend, zrecv, csend, crecv, psend, precv, gsend, grecv, fsend, frecv, local,
):
    me = Place()
    across = (me.pipe, me.across)
    mirror = (7 - me.pipe, me.expert)
    mirror_across = (7 - me.pipe, me.across)
    a_to = lax.rem(me.pipe + 1, 8)
    a_from = lax.rem(me.pipe + 7, 8)
    b_to = lax.rem(8 - me.pipe, 8)
    stays = b_to == me.pipe
    barrier = pltpu.get_barrier_semaphore()
    greet = [me.plane(me.spot_at(i, j)) for i, j in NEAR] + [across, mirror, mirror_across]
    greet += [(a_to, me.expert), (a_to, me.across), (a_from, me.expert), (a_from, me.across), (b_to, me.across)]
    for device in greet:
        pl.semaphore_signal(barrier, inc=1, device_id=device, device_id_type=MESH)

    @pl.when(jnp.logical_not(stays))
    def _():
        pl.semaphore_signal(barrier, inc=1, device_id=(b_to, me.expert), device_id_type=MESH)

    loads = [
        pltpu.make_async_copy(ax, own_a, local.at[0]),
        pltpu.make_async_copy(up_in, up, local.at[1]),
        pltpu.make_async_copy(down_in, down, local.at[2]),
    ]
    for copy in loads:
        copy.start()
    pl.semaphore_wait(barrier, len(greet) + 1 - stays.astype(jnp.int32))

    small = []
    for i, (row, col, to) in enumerate(
        ((acode, acol, across), (bcode, bcol, mirror), (bcode, bcol, mirror_across))
    ):
        small += [
            remote(row, codes.at[i], csend.at[i], crecv.at[i], to),
            remote(col, code_cols.at[i], csend.at[3 + i], crecv.at[3 + i], to),
        ]
    for copy in small:
        copy.start()

    def z_copy(lane, q):
        src, dst, to = [
            (ax, far_a, across),
            (bx, got_b.at[0], mirror),
            (bx, got_b.at[1], mirror_across),
            (bc, got_b.at[2], mirror),
            (bc, got_b.at[3], mirror_across),
        ][lane]
        return remote(src.at[:, cols(q)], dst.at[:, cols(q)], zsend.at[lane, q], zrecv.at[lane, q], to)

    for lanes in ((0,), (1, 2), (3, 4)):
        @pl.loop(0, PARTS)
        def _(q):
            for lane in lanes:
                z_copy(lane, q).start()

    def spread(t, send, recv, at):
        pltpu.make_async_copy(
            send.at[rows16(me.spot // 2), cols(at)], recv.at[me.spot, :, cols(at)], precv.at[t]
        ).start()
        for i, j in NEAR:
            to = me.spot_at(i, j)
            remote(
                send.at[rows16(to // 2), cols(at)], recv.at[me.spot, :, cols(at)],
                psend.at[t], precv.at[t], me.plane(to),
            ).start()

    def spread_back(t, send, recv, at, sem):
        pltpu.make_async_copy(
            send.at[me.spot, :, cols(at)], recv.at[me.spot, :, cols(at)], grecv.at[t, sem]
        ).start()
        for i, j in NEAR:
            to = me.spot_at(i, j)
            remote(
                send.at[to, :, cols(at)], recv.at[me.spot, :, cols(at)],
                gsend.at[t], grecv.at[t, sem], me.plane(to),
            ).start()

    def arrived(ref, sem):
        pltpu.make_async_copy(ref, ref, sem).wait()

    def block(ref, at):
        return ref[:, :, cols(at)].reshape(PLANE * 16, W)

    def put(ref, at, value):
        ref[:, :, cols(at)] = value.reshape(PLANE, 16, W)

    recvs = (ra, rbx, rbc)
    sets = ((0, 256), (256, 256), (512, TAIL))

    def rows_of(t, s, q):
        return block(recvs[t], PARTS * s + q) if s < 2 else tails[t, :, cols(q)]

    def put_rows(t, s, q, value):
        if s < 2:
            put(recvs[t], PARTS * s + q, value)
        else:
            tails[t, :, cols(q)] = value

    def pick_tail(t):
        @pl.loop(0, PARTS)
        def _(q):
            tails[t, :, cols(q)] = dot(gather_tail(q), block(recvs[t], 2 * PARTS)).astype(BF)

    def put_tail(ret):
        left_ret = dot(spread_tail(0), tail_ret[:, cols(0)])
        for q in range(1, PARTS):
            left_ret += dot(spread_tail(q), tail_ret[:, cols(q)])
        put(ret, 2 * PARTS, left_ret.astype(BF))

    def norm_rows(t, s):
        at, n = sets[s]
        rows = pl.ds(at, n)
        stat[0, rows] = jnp.zeros((n, 1), jnp.float32)
        stat[1, rows] = jnp.zeros((n, 1), jnp.float32)
        hidden[rows] = jnp.zeros((n, HID), jnp.float32)

        @pl.loop(0, PARTS)
        def _(q):
            x = rows_of(t, s, q).astype(jnp.float32)
            stat[0, rows] += jnp.sum(x * x, axis=1, keepdims=True)

        stat[0, rows] = lax.rsqrt(stat[0, rows] / D + EPS)

        @pl.loop(0, PARTS)
        def _(q):
            normed = (rows_of(t, s, q).astype(jnp.float32) * stat[0, rows]).astype(BF)
            put_rows(t, s, q, normed)
            hidden[rows] += dot(normed, up[part_rows(q)])
            stat[1, rows] += jnp.sum(normed.astype(jnp.float32) * column[0:1, cols(q)], axis=1, keepdims=True)

        stat[2, rows] = jax.nn.sigmoid(stat[1, rows])

    def forward_rows(s):
        at, n = sets[s]
        rows = pl.ds(at, n)
        norm_rows(0, s)
        h = hidden[rows]
        act[rows] = (h * jax.nn.sigmoid(h)).astype(BF)

        @pl.loop(0, PARTS)
        def _(q):
            value = (stat[2, rows] * dot(act[rows], down[:, cols(q)])).astype(BF)
            if s < 2:
                put(ret_a, PARTS * s + q, value)
            else:
                tail_ret[:, cols(q)] = value

    def gate_rows(s):
        at, n = sets[s]
        rows = pl.ds(at, n)
        act_grad[rows] = jnp.zeros((n, HID), jnp.float32)

        @pl.loop(0, PARTS)
        def _(q):
            cot = (rows_of(2, s, q).astype(jnp.float32) * stat[2, rows]).astype(BF)
            put_rows(2, s, q, cot)
            act_grad[rows] += dot_nt(cot, down[:, cols(q)])

        h, g = hidden[rows], act_grad[rows]
        sig = jax.nn.sigmoid(h)
        a = (h * sig).astype(BF)
        act[rows] = a
        hg = (g * sig * (1.0 + h * (1.0 - sig))).astype(BF)
        hid_grad[rows] = hg
        score_part = jnp.sum(a.astype(jnp.float32) * g, axis=1, keepdims=True) * (1.0 - stat[2, rows])
        stat[3, rows] = score_part
        along = jnp.sum(hg.astype(jnp.float32) * h, axis=1, keepdims=True) + score_part * stat[1, rows]
        stat[4, rows] = along / D

    def back_rows(s, q):
        at, n = sets[s]
        rows = pl.ds(at, n)
        grad = dot_nt(hid_grad[rows], up[part_rows(q)]) + stat[3, rows] * column[0:1, cols(q)]
        value = stat[0, rows] * (grad - rows_of(1, s, q).astype(jnp.float32) * stat[4, rows])
        if s < 2:
            put(ret_b, PARTS * s + q, value.astype(BF))
        else:
            tail_ret[:, cols(q)] = value.astype(BF)

    loads[0].wait()
    sel[0, 0] = selector("own0", acode[0:1, :])

    @pl.loop(0, PARTS)
    def _(q):
        send_a[:, cols(q)] = dot(sel[0, 0], own_a[:, cols(q)]).astype(BF)
        spread(0, send_a, ra, q)

    small[0].wait()
    small[1].wait()
    fill_selectors(selector, sel, 0, acode[0:1, :], codes[0, 0:1, :])
    left[...] = jnp.zeros_like(left)

    @pl.loop(0, PARTS)
    def _(q):
        z_copy(0, q).wait()
        there = far_a[:, cols(q)]
        send_a[:, cols(PARTS + q)] = (dot(sel[0, 1], own_a[:, cols(q)]) + dot(sel[0, 2], there)).astype(BF)
        left[...] += dot(sel[0, 3 + q], there)
        spread(0, send_a, ra, PARTS + q)

    send_a[:, 2 * D:] = left[...].astype(BF)
    spread(0, send_a, ra, 2 * PARTS)

    for copy in small[2:]:
        copy.wait()
    fill_selectors(selector, sel, 1, codes[1, 0:1, :], codes[2, 0:1, :])

    def slot_part(t, send, recv, q):
        z_copy(2 * t - 1, q).wait()
        here = got_b[2 * t - 2, :, cols(q)]
        send[:, cols(q)] = dot(sel[1, 0], here).astype(BF)
        spread(t, send, recv, q)
        z_copy(2 * t, q).wait()
        there = got_b[2 * t - 1, :, cols(q)]
        send[:, cols(PARTS + q)] = (dot(sel[1, 1], here) + dot(sel[1, 2], there)).astype(BF)
        left[...] += dot(sel[1, 3 + q], there)
        spread(t, send, recv, PARTS + q)

    left[...] = jnp.zeros_like(left)

    @pl.loop(0, PARTS)
    def _(q):
        slot_part(1, send_bx, rbx, q)

    send_bx[:, 2 * D:] = left[...].astype(BF)
    spread(1, send_bx, rbx, 2 * PARTS)

    left[...] = jnp.zeros_like(left)
    loads[1].wait()
    loads[2].wait()
    arrived(ra, precv.at[0])
    for q in range(PARTS):
        if q == 0:
            pick_tail(0)
            forward_rows(2)
            put_tail(ret_a)
        if q in (1, 2):
            forward_rows(q - 1)
        slot_part(2, send_bc, rbc, q)
    send_bc[:, 2 * D:] = left[...].astype(BF)
    spread(2, send_bc, rbc, 2 * PARTS)

    spread_back(0, ret_a, ga, 2 * PARTS, PARTS)

    @pl.loop(0, PARTS)
    def _(q):
        spread_back(0, ret_a, ga, PARTS + q, q)
        spread_back(0, ret_a, ga, q, q)

    fill_selectors(unselector, sums, 0, acol[:, 0:1], code_cols[0, :, 0:1])
    fill_selectors(unselector, sums, 1, code_cols[1, :, 0:1], code_cols[2, :, 0:1])

    arrived(rbx, precv.at[1])
    pick_tail(1)
    for s in (2, 0, 1):
        norm_rows(1, s)
    arrived(rbc, precv.at[2])
    pick_tail(2)
    for s in (2, 0, 1):
        gate_rows(s)
        if s == 2:
            @pl.loop(0, PARTS)
            def _(q):
                back_rows(2, q)

            put_tail(ret_b)
            spread_back(1, ret_b, gb, 2 * PARTS, PARTS)

    @pl.loop(0, PARTS)
    def _(q):
        back_rows(1, q)
        spread_back(1, ret_b, gb, PARTS + q, q)
        back_rows(0, q)
        spread_back(1, ret_b, gb, q, q)

    def far_copy(t, out, to, q):
        return remote(
            far.at[t, :, cols(q)], out.at[1, :, cols(q)], fsend.at[t, 1, q], frecv.at[t, 1, q], (to, me.across)
        )

    def own_copy(t, out, to, q):
        return remote(
            own.at[t, :, cols(q)], out.at[0, :, cols(q)], fsend.at[t, 0, q], frecv.at[t, 0, q], (to, me.expert)
        )

    def own_stay(t, out, q):
        return pltpu.make_async_copy(own.at[t, :, cols(q)], out.at[0, :, cols(q)], frecv.at[t, 0, q])

    def collect(t, recv, base, out, to):
        arrived(recv.at[:, :, pl.ds(2 * D, W)], grecv.at[t, PARTS])

        @pl.loop(0, PARTS)
        def _(q):
            arrived(recv.at[:, :, pl.ds(0, 2 * W)], grecv.at[t, q])
            second = block(recv, PARTS + q)
            far[t, :, cols(q)] = (
                dot(sums[t, 2], second) + dot(sums[t, 3 + q], block(recv, 2 * PARTS))
            ).astype(BF)
            far_copy(t, out, to, q).start()
            own[t, :, cols(q)] = (
                base[:, cols(q)].astype(jnp.float32) + dot(sums[t, 0], block(recv, q)) + dot(sums[t, 1], second)
            ).astype(BF)
            if t == 0:
                own_copy(t, out, to, q).start()
            else:
                @pl.when(stays)
                def _():
                    own_stay(t, out, q).start()

                @pl.when(jnp.logical_not(stays))
                def _():
                    own_copy(t, out, to, q).start()

    collect(0, ga, own_a, oa, a_to)

    @pl.loop(0, PARTS)
    def _(q):
        total = dot_tn(act[pl.ds(0, 256)], rows_of(2, 0, q))
        total += dot_tn(act[pl.ds(256, 256)], rows_of(2, 1, q))
        total += dot_tn(act[pl.ds(512, TAIL)], rows_of(2, 2, q))
        down_grad[:, cols(q)] = total.astype(BF)
        total = dot_tn(rows_of(1, 0, q), hid_grad[pl.ds(0, 256)])
        total += dot_tn(rows_of(1, 1, q), hid_grad[pl.ds(256, 256)])
        total += dot_tn(rows_of(1, 2, q), hid_grad[pl.ds(512, TAIL)])
        up_grad[part_rows(q)] = total.astype(BF)

    stores = [
        pltpu.make_async_copy(up_grad, up_out, local.at[3]),
        pltpu.make_async_copy(down_grad, down_out, local.at[4]),
    ]
    for copy in stores:
        copy.start()

    collect(1, gb, got_b.at[2], ob, b_to)

    for t, recv in enumerate(recvs):
        most = recv.at[pl.ds(0, PLANE - 1)]
        remote(most, most, psend.at[t], precv.at[t], across).wait_send()
    for t, recv, out, to in ((0, ga, oa, a_to), (1, gb, ob, b_to)):
        most = recv.at[pl.ds(0, PLANE - 1)]
        remote(most, most, gsend.at[t], grecv.at[t, 0], across).wait_send()

        @pl.loop(0, PARTS)
        def _(q):
            far_copy(t, out, to, q).wait()
            if t == 0:
                own_copy(t, out, to, q).wait()
            else:
                @pl.when(jnp.logical_not(stays))
                def _():
                    own_copy(t, out, to, q).wait()

                @pl.when(stays)
                def _():
                    own_stay(t, out, q).wait()
    for copy in stores:
        copy.wait()


def span(*operands):
    anywhere = pl.BlockSpec(memory_space=pl.ANY)
    inside = pl.BlockSpec(memory_space=pltpu.VMEM)
    dma = pltpu.SemaphoreType.DMA
    pair = jax.ShapeDtypeStruct((2, TOK, D), BF)

    def held(*shape, kind=BF):
        return pltpu.VMEM(shape, kind)

    return pl.pallas_call(
        span_kernel,
        name="span",
        out_shape=(pair, pair, jax.ShapeDtypeStruct((D, HID), BF), jax.ShapeDtypeStruct((HID, D), BF)),
        in_specs=[anywhere] * 3 + [inside] * 4 + [anywhere] * 2 + [inside],
        out_specs=(anywhere,) * 4,
        scratch_shapes=[
            held(TOK, D), held(TOK, D), held(4, TOK, D),
            held(3, 8, TOK, kind=jnp.int32), held(3, TOK, TOK, kind=jnp.int32),
            held(TOK, WIDE), held(TOK, WIDE), held(TOK, WIDE),
            held(PLANE, 16, WIDE), held(PLANE, 16, WIDE), held(PLANE, 16, WIDE),
            held(PLANE, 16, WIDE), held(PLANE, 16, WIDE), held(PLANE, 16, WIDE), held(PLANE, 16, WIDE),
            held(2, TOK, D), held(2, TOK, D), held(D, HID), held(HID, D), held(D, HID), held(HID, D),
            held(TOK, W, kind=jnp.float32), held(2, 3 + PARTS, TOK, TOK), held(2, 3 + PARTS, TOK, PLANE * 16),
            held(3, TAIL, D), held(TAIL, D),
            held(ROWS, HID, kind=jnp.float32), held(ROWS, HID, kind=jnp.float32),
            held(ROWS, HID), held(ROWS, HID), held(5, ROWS, 1, kind=jnp.float32),
            dma((5, PARTS)), dma((5, PARTS)), dma((6,)), dma((6,)), dma((3,)), dma((3,)),
            dma((2,)), dma((2, PARTS + 1)), dma((2, 2, PARTS)), dma((2, 2, PARTS)), dma((5,)),
        ],
        compiler_params=pltpu.CompilerParams(collective_id=1, has_side_effects=True, vmem_limit_bytes=67043328),
    )(*operands)


def slot_code(route):
    ids = route.reshape(TOK)
    same = ids[:, None] == ids[None, :]
    earlier = jnp.arange(TOK)[:, None] < jnp.arange(TOK)[None, :]
    slot = jnp.sum((same & earlier).astype(jnp.int32), axis=0)
    return (ids * 32 + slot).astype(jnp.int32)


def body(a_input, a_route, b_saved, b_grad, b_route, up_weight, down_weight, router):
    group = lax.axis_size("expert") // EXPERTS
    mine = lax.axis_index("expert") // group
    column = lax.dynamic_slice(router[0], (0, mine), (D, 1))[:, 0].astype(jnp.float32)
    codes = [slot_code(a_route[0]), slot_code(b_route[0])]
    out_a, out_b, up_grad, down_grad = span(
        a_input[0], b_saved[0], b_grad[0],
        *[jnp.broadcast_to(c[None, :], (8, TOK)) for c in codes],
        *[jnp.broadcast_to(c[:, None], (TOK, TOK)) for c in codes],
        up_weight[0], down_weight[0], jnp.broadcast_to(column[None, :], (8, D)),
    )
    a_next = (out_a[0].astype(jnp.float32) + out_a[1].astype(jnp.float32)).astype(BF)
    b_next = (out_b[0].astype(jnp.float32) + out_b[1].astype(jnp.float32)).astype(BF)
    return a_next[None], b_next[None], up_grad[None], down_grad[None]


def solution(mesh):
    rows = P("pipe", "expert", None)
    return jax.shard_map(
        body,
        mesh=mesh,
        in_specs=(rows, rows, rows, rows, rows, P("pipe", None, "expert"), rows, P("pipe", None, None)),
        out_specs=(rows, rows, P("pipe", None, "expert"), rows),
        check_vma=False,
    )
```

```python
import jax
import jax.numpy as jnp
from jax import lax
from jax.experimental import pallas as pl
from jax.experimental.pallas import tpu as pltpu
from jax.sharding import PartitionSpec as P

EPS = 1e-06
MESH = pl.DeviceIdType.MESH
TOK = 128
D = 3584
CAP = 18
EXPERTS = 8
SIDE = 4
GROUP = 8
PARTS = 4
W = D // PARTS
WIDE = 9 * W
HALF = 256
HID = 2 * HALF
LINES = GROUP * 16
TAIL = GROUP * 4
ROWS = 2 * LINES + TAIL
BF = jnp.bfloat16
NEAR = sorted(
    [(i, j) for i in range(SIDE) for j in range(2) if i or j], key=lambda s: min(s[0], SIDE - s[0]) + s[1]
)


class Place:
    def __init__(self):
        self.pipe = lax.axis_index("pipe")
        self.expert = lax.axis_index("expert")
        self.half = lax.rem(self.expert, 2)
        self.x = self.expert // 8
        self.y = lax.rem(self.expert // 2, SIDE)
        self.across = self.expert + 1 - 2 * self.half
        self.mine = self.expert // 4
        self.twin = (self.pipe, self.expert + 2 - 4 * lax.rem(self.y, 2))

    def peer(self, dx, flip):
        x = lax.rem(self.x + dx, SIDE)
        y = 3 - self.y if flip else self.y
        return x, x * 2 + y // 2, (self.pipe, x * 8 + y * 2 + self.half)


def remote(src, dst, send, recv, device):
    return pltpu.make_async_remote_copy(
        src_ref=src, dst_ref=dst, send_sem=send, recv_sem=recv, device_id=device, device_id_type=MESH
    )


def cols(at, width=W):
    return pl.ds(pl.multiple_of(at * W, 128), width)


def part_rows(q):
    return pl.ds(pl.multiple_of(q * W, 128), W)


def rows16(e):
    return pl.ds(pl.multiple_of(e * 16, 16), 16)


def selector(kind, code, part=0):
    row = lax.broadcasted_iota(jnp.int32, (TOK, TOK), 0)
    return ((row == code // 32 * 16 + place(kind, code % 32, part)) & allowed(kind, code % 32)).astype(jnp.float32).astype(BF)


def place(kind, slot, part):
    return {"own0": slot, "own1": slot - 16, "far1": slot + 2, "left": slot - 14 + 4 * part}[kind]


def allowed(kind, slot):
    return {"own0": slot < 16, "own1": slot >= 16, "far1": slot < 14, "left": slot >= 14}[kind]


def unselector(kind, code, part=0):
    lane = lax.broadcasted_iota(jnp.int32, (TOK, LINES), 1)
    slot = code % 32
    hit = (lane // 16 == code // 32) & (lane % 16 == place(kind, slot, part)) & allowed(kind, slot)
    return hit.astype(jnp.float32).astype(BF)


def fill_selectors(make, sel, t, own_code, far_code):
    sel[t, 0] = make("own0", own_code)
    sel[t, 1] = make("own1", own_code)
    sel[t, 2] = make("far1", far_code)
    for q in range(PARTS):
        sel[t, 3 + q] = make("left", far_code, q)


def codes_of(ids):
    i = lax.broadcasted_iota(jnp.int32, (TOK, TOK), 0)
    j = lax.broadcasted_iota(jnp.int32, (TOK, TOK), 1)
    wide = jnp.broadcast_to(ids, (TOK, TOK))
    col = jnp.sum(jnp.where(i == j, wide, 0).astype(jnp.float32), axis=1, keepdims=True).astype(jnp.int32)
    same = col == wide
    slot_row = jnp.sum(jnp.where(same & (i < j), 1.0, 0.0), axis=0, keepdims=True).astype(jnp.int32)
    slot_col = jnp.sum(jnp.where(same & (j < i), 1.0, 0.0), axis=1, keepdims=True).astype(jnp.int32)
    return ids * 32 + slot_row, col * 32 + slot_col


def dot(a, b):
    return jnp.dot(a, b, preferred_element_type=jnp.float32)


def dot_nt(a, b):
    return lax.dot_general(a, b, (((1,), (1,)), ((), ())), preferred_element_type=jnp.float32)


def dot_tn(a, b):
    return lax.dot_general(a, b, (((0,), (0,)), ((), ())), preferred_element_type=jnp.float32)


def gather_tail(q):
    r = lax.broadcasted_iota(jnp.int32, (TAIL, LINES), 0)
    c = lax.broadcasted_iota(jnp.int32, (TAIL, LINES), 1)
    return ((c // 16 == r // 4) & (c % 16 == 4 * q + r % 4)).astype(jnp.float32).astype(BF)


def spread_tail(q):
    c = lax.broadcasted_iota(jnp.int32, (LINES, TAIL), 0)
    r = lax.broadcasted_iota(jnp.int32, (LINES, TAIL), 1)
    return ((c // 16 == r // 4) & (c % 16 == 4 * q + r % 4)).astype(jnp.float32).astype(BF)


def span_kernel(
    ax, bx, bc, a_ids, b_ids, up_in, down_in, column,
    oa, ob, up_out, down_out,
    own_a, far_a, got_b, ids, send_a, send_bx, send_bc, ra, rbx, rbc,
    ret_a, ret_b, ga, gb, own, far, up, down, up_own, up_far, down_own, down_far,
    left, sel, sums, tails, tail_ret, hidden, act_grad, act, act_a, hid_grad, stat,
    zsend, zrecv, csend, crecv, psend, precv, gsend, grecv, fsend, frecv, wsend, wrecv, dsend, drecv, local,
):
    me = Place()
    across = (me.pipe, me.across)
    mirror = (7 - me.pipe, me.expert)
    mirror_across = (7 - me.pipe, me.across)
    a_to = lax.rem(me.pipe + 1, 8)
    a_from = lax.rem(me.pipe + 7, 8)
    b_to = lax.rem(8 - me.pipe, 8)
    stays = b_to == me.pipe
    barrier = pltpu.get_barrier_semaphore()
    greet = [me.peer(i, j)[2] for i, j in NEAR] + [me.twin, across, mirror, mirror_across]
    greet += [(a_to, me.expert), (a_to, me.across), (a_from, me.expert), (a_from, me.across), (b_to, me.across)]
    for device in greet:
        pl.semaphore_signal(barrier, inc=1, device_id=device, device_id_type=MESH)

    @pl.when(jnp.logical_not(stays))
    def _():
        pl.semaphore_signal(barrier, inc=1, device_id=(b_to, me.expert), device_id_type=MESH)

    loads = [
        pltpu.make_async_copy(ax, own_a, local.at[0]),
        pltpu.make_async_copy(up_in, up.at[:, pl.ds(0, HALF)], local.at[1]),
        pltpu.make_async_copy(down_in, down.at[pl.ds(0, HALF)], local.at[2]),
    ]
    for copy in loads:
        copy.start()
    pl.semaphore_wait(barrier, len(greet) + 1 - stays.astype(jnp.int32))

    small = [
        remote(src, ids.at[i], csend.at[i], crecv.at[i], to)
        for i, (src, to) in enumerate(((a_ids, across), (b_ids, mirror), (b_ids, mirror_across)))
    ]
    weights = [
        remote(up_in, up.at[:, pl.ds(HALF, HALF)], wsend.at[0], wrecv.at[0], me.twin),
        remote(down_in, down.at[pl.ds(HALF, HALF)], wsend.at[1], wrecv.at[1], me.twin),
    ]
    for copy in small + weights:
        copy.start()

    def z_copy(lane, q):
        src, dst, to = [
            (ax, far_a, across),
            (bx, got_b.at[0], mirror),
            (bx, got_b.at[1], mirror_across),
            (bc, got_b.at[2], mirror),
            (bc, got_b.at[3], mirror_across),
        ][lane]
        return remote(src.at[:, cols(q)], dst.at[:, cols(q)], zsend.at[lane, q], zrecv.at[lane, q], to)

    for lanes in ((1, 2), (3, 4), (0,)):
        @pl.loop(0, PARTS)
        def _(q):
            for lane in lanes:
                z_copy(lane, q).start()

    def spread(t, send, recv, at):
        pltpu.make_async_copy(
            send.at[rows16(me.mine), cols(at)], recv.at[me.x * 2, :, cols(at)], precv.at[t]
        ).start()
        for i, j in NEAR:
            x, e, device = me.peer(i, j)
            remote(
                send.at[rows16(e), cols(at)], recv.at[me.x * 2 + j, :, cols(at)], psend.at[t], precv.at[t], device
            ).start()

    def spread_back(t, send, recv, at, sem):
        pltpu.make_async_copy(
            send.at[me.x * 2, :, cols(at)], recv.at[me.mine, :, cols(at)], grecv.at[t, sem]
        ).start()
        for i, j in NEAR:
            x, e, device = me.peer(i, j)
            remote(
                send.at[x * 2 + j, :, cols(at)], recv.at[me.mine, :, cols(at)], gsend.at[t], grecv.at[t, sem], device
            ).start()

    def arrived(ref, sem):
        pltpu.make_async_copy(ref, ref, sem).wait()

    def block(ref, at):
        return ref[:, :, cols(at)].reshape(LINES, W)

    def put(ref, at, value):
        ref[:, :, cols(at)] = value.reshape(GROUP, 16, W)

    recvs = (ra, rbx, rbc)
    sets = ((0, LINES), (LINES, LINES), (2 * LINES, TAIL))

    def rows_of(t, s, q):
        return block(recvs[t], PARTS * s + q) if s < 2 else tails[t, :, cols(q)]

    def put_rows(t, s, q, value):
        if s < 2:
            put(recvs[t], PARTS * s + q, value)
        else:
            tails[t, :, cols(q)] = value

    def pick_tail(t):
        @pl.loop(0, PARTS)
        def _(q):
            tails[t, :, cols(q)] = dot(gather_tail(q), block(recvs[t], 2 * PARTS)).astype(BF)

    def put_tail(ret):
        left_ret = dot(spread_tail(0), tail_ret[:, cols(0)])
        for q in range(1, PARTS):
            left_ret += dot(spread_tail(q), tail_ret[:, cols(q)])
        put(ret, 2 * PARTS, left_ret.astype(BF))

    def norm_rows(t, s):
        at, n = sets[s]
        rows = pl.ds(at, n)
        stat[0, rows] = jnp.zeros((n, 1), jnp.float32)
        stat[1, rows] = jnp.zeros((n, 1), jnp.float32)
        hidden[rows] = jnp.zeros((n, HID), jnp.float32)

        @pl.loop(0, PARTS)
        def _(q):
            x = rows_of(t, s, q).astype(jnp.float32)
            stat[0, rows] += jnp.sum(x * x, axis=1, keepdims=True)

        stat[0, rows] = lax.rsqrt(stat[0, rows] / D + EPS)

        @pl.loop(0, PARTS)
        def _(q):
            normed = (rows_of(t, s, q).astype(jnp.float32) * stat[0, rows]).astype(BF)
            put_rows(t, s, q, normed)
            hidden[rows] += dot(normed, up[part_rows(q)])
            stat[1, rows] += jnp.sum(normed.astype(jnp.float32) * column[0:1, cols(q)], axis=1, keepdims=True)

        stat[2, rows] = jax.nn.sigmoid(stat[1, rows])

    def forward_rows(s):
        at, n = sets[s]
        rows = pl.ds(at, n)
        norm_rows(0, s)
        h = hidden[rows]
        act_a[rows] = (h * jax.nn.sigmoid(h)).astype(BF)

    def out_rows(s, q):
        at, n = sets[s]
        rows = pl.ds(at, n)
        value = (stat[2, rows] * dot(act_a[rows], down[:, cols(q)])).astype(BF)
        if s < 2:
            put(ret_a, PARTS * s + q, value)
        else:
            tail_ret[:, cols(q)] = value

    def gate_rows(s):
        at, n = sets[s]
        rows = pl.ds(at, n)
        act_grad[rows] = jnp.zeros((n, HID), jnp.float32)

        @pl.loop(0, PARTS)
        def _(q):
            cot = (rows_of(2, s, q).astype(jnp.float32) * stat[2, rows]).astype(BF)
            put_rows(2, s, q, cot)
            act_grad[rows] += dot_nt(cot, down[:, cols(q)])

        h, g = hidden[rows], act_grad[rows]
        sig = jax.nn.sigmoid(h)
        a = (h * sig).astype(BF)
        act[rows] = a
        hg = (g * sig * (1.0 + h * (1.0 - sig))).astype(BF)
        hid_grad[rows] = hg
        score_part = jnp.sum(a.astype(jnp.float32) * g, axis=1, keepdims=True) * (1.0 - stat[2, rows])
        stat[3, rows] = score_part
        along = jnp.sum(hg.astype(jnp.float32) * h, axis=1, keepdims=True) + score_part * stat[1, rows]
        stat[4, rows] = along / D

    def back_rows(s, q):
        at, n = sets[s]
        rows = pl.ds(at, n)
        grad = dot_nt(hid_grad[rows], up[part_rows(q)]) + stat[3, rows] * column[0:1, cols(q)]
        value = stat[0, rows] * (grad - rows_of(1, s, q).astype(jnp.float32) * stat[4, rows])
        if s < 2:
            put(ret_b, PARTS * s + q, value.astype(BF))
        else:
            tail_ret[:, cols(q)] = value.astype(BF)

    def far_copy(t, out, to, q):
        return remote(
            far.at[t, :, cols(q)], out.at[1, :, cols(q)], fsend.at[t, 1, q], frecv.at[t, 1, q], (to, me.across)
        )

    def own_copy(t, out, to, q):
        return remote(
            own.at[t, :, cols(q)], out.at[0, :, cols(q)], fsend.at[t, 0, q], frecv.at[t, 0, q], (to, me.expert)
        )

    def own_stay(t, out, q):
        return pltpu.make_async_copy(own.at[t, :, cols(q)], out.at[0, :, cols(q)], frecv.at[t, 0, q])

    ends = ((ga, own_a, oa, a_to), (gb, got_b.at[2], ob, b_to))

    def collect_edge(t):
        arrived(ends[t][0].at[:, :, pl.ds(2 * D, W)], grecv.at[t, PARTS])

    def collect(t, q):
        recv, base, out, to = ends[t]
        arrived(recv.at[:, :, pl.ds(0, 2 * W)], grecv.at[t, q])
        second = block(recv, PARTS + q)
        far[t, :, cols(q)] = (dot(sums[t, 2], second) + dot(sums[t, 3 + q], block(recv, 2 * PARTS))).astype(BF)
        far_copy(t, out, to, q).start()
        own[t, :, cols(q)] = (
            base[:, cols(q)].astype(jnp.float32) + dot(sums[t, 0], block(recv, q)) + dot(sums[t, 1], second)
        ).astype(BF)
        if t == 0:
            own_copy(t, out, to, q).start()
        else:
            @pl.when(stays)
            def _():
                own_stay(t, out, q).start()

            @pl.when(jnp.logical_not(stays))
            def _():
                own_copy(t, out, to, q).start()

    def down_part(at, q):
        total = 0.0
        for s, (first, n) in enumerate(sets):
            total += dot_tn(act[pl.ds(first, n), pl.ds(at, HALF)], rows_of(2, s, q))
        return total.astype(BF)

    def up_part(at, q):
        total = 0.0
        for s, (first, n) in enumerate(sets):
            total += dot_tn(rows_of(1, s, q), hid_grad[pl.ds(first, n), pl.ds(at, HALF)])
        return total.astype(BF)

    def grad_copies(q):
        return [
            remote(down_far.at[:, cols(q)], down_out.at[1, :, cols(q)], dsend.at[0, q], drecv.at[0, q], me.twin),
            remote(up_far.at[part_rows(q)], up_out.at[1, part_rows(q)], dsend.at[1, q], drecv.at[1, q], me.twin),
        ]

    a_row, a_col = codes_of(a_ids[...])
    sel[0, 0] = selector("own0", a_row)
    loads[0].wait()

    @pl.loop(0, PARTS)
    def _(q):
        send_a[:, cols(q)] = dot(sel[0, 0], own_a[:, cols(q)]).astype(BF)
        spread(0, send_a, ra, q)

    for copy in small:
        copy.wait()
    b_row, b_col = codes_of(ids[1])
    b_far_row, b_far_col = codes_of(ids[2])
    fill_selectors(selector, sel, 1, b_row, b_far_row)

    for t, send, recv in ((1, send_bx, rbx), (2, send_bc, rbc)):
        left[...] = jnp.zeros_like(left)

        @pl.loop(0, PARTS)
        def _(q):
            z_copy(2 * t - 1, q).wait()
            here = got_b[2 * t - 2, :, cols(q)]
            send[:, cols(q)] = dot(sel[1, 0], here).astype(BF)
            spread(t, send, recv, q)
            z_copy(2 * t, q).wait()
            there = got_b[2 * t - 1, :, cols(q)]
            send[:, cols(PARTS + q)] = (dot(sel[1, 1], here) + dot(sel[1, 2], there)).astype(BF)
            left[...] += dot(sel[1, 3 + q], there)
            spread(t, send, recv, PARTS + q)

        send[:, 2 * D:] = left[...].astype(BF)
        spread(t, send, recv, 2 * PARTS)
        if t == 1:
            a_far_row, a_far_col = codes_of(ids[0])
            fill_selectors(selector, sel, 0, a_row, a_far_row)
            fill_selectors(unselector, sums, 0, a_col, a_far_col)
            fill_selectors(unselector, sums, 1, b_col, b_far_col)

    for copy in loads[1:] + weights:
        copy.wait()
    arrived(rbx, precv.at[1])
    pick_tail(1)
    for s in (2, 0, 1):
        norm_rows(1, s)
    arrived(rbc, precv.at[2])
    pick_tail(2)
    for s in (2, 0, 1):
        gate_rows(s)
        if s == 2:
            @pl.loop(0, PARTS)
            def _(q):
                back_rows(2, q)

            put_tail(ret_b)
            spread_back(1, ret_b, gb, 2 * PARTS, PARTS)

    @pl.loop(0, PARTS)
    def _(q):
        back_rows(1, q)
        spread_back(1, ret_b, gb, PARTS + q, q)
        back_rows(0, q)
        spread_back(1, ret_b, gb, q, q)

    @pl.loop(0, PARTS)
    def _(q):
        down_far[:, cols(q)] = down_part(HALF, q)
        up_far[part_rows(q)] = up_part(HALF, q)
        for copy in grad_copies(q):
            copy.start()

    left[...] = jnp.zeros_like(left)
    for q in range(PARTS):
        if q == PARTS - 1:
            collect_edge(1)
            collect(1, 0)
        z_copy(0, q).wait()
        there = far_a[:, cols(q)]
        send_a[:, cols(PARTS + q)] = (dot(sel[0, 1], own_a[:, cols(q)]) + dot(sel[0, 2], there)).astype(BF)
        left[...] += dot(sel[0, 3 + q], there)
        spread(0, send_a, ra, PARTS + q)

    send_a[:, 2 * D:] = left[...].astype(BF)
    spread(0, send_a, ra, 2 * PARTS)

    @pl.loop(1, PARTS)
    def _(q):
        collect(1, q)

    arrived(ra, precv.at[0])
    pick_tail(0)
    forward_rows(2)

    @pl.loop(0, PARTS)
    def _(q):
        out_rows(2, q)

    put_tail(ret_a)
    spread_back(0, ret_a, ga, 2 * PARTS, PARTS)
    forward_rows(1)
    forward_rows(0)

    @pl.loop(0, PARTS)
    def _(q):
        out_rows(1, q)
        spread_back(0, ret_a, ga, PARTS + q, q)
        out_rows(0, q)
        spread_back(0, ret_a, ga, q, q)

    @pl.loop(0, PARTS)
    def _(q):
        down_own[:, cols(q)] = down_part(0, q)
        up_own[part_rows(q)] = up_part(0, q)

    stores = [
        pltpu.make_async_copy(up_own, up_out.at[0], local.at[3]),
        pltpu.make_async_copy(down_own, down_out.at[0], local.at[4]),
    ]
    for copy in stores:
        copy.start()

    collect_edge(0)

    @pl.loop(0, PARTS)
    def _(q):
        collect(0, q)

    for t, recv in enumerate(recvs):
        most = recv.at[pl.ds(0, GROUP - 1)]
        remote(most, most, psend.at[t], precv.at[t], across).wait_send()
    for t, (recv, base, out, to) in enumerate(ends):
        most = recv.at[pl.ds(0, GROUP - 1)]
        remote(most, most, gsend.at[t], grecv.at[t, 0], across).wait_send()

        @pl.loop(0, PARTS)
        def _(q):
            far_copy(t, out, to, q).wait()
            if t == 0:
                own_copy(t, out, to, q).wait()
                for copy in grad_copies(q):
                    copy.wait()
            else:
                @pl.when(jnp.logical_not(stays))
                def _():
                    own_copy(t, out, to, q).wait()

                @pl.when(stays)
                def _():
                    own_stay(t, out, q).wait()
    for copy in stores:
        copy.wait()


def span(*operands):
    anywhere = pl.BlockSpec(memory_space=pl.ANY)
    inside = pl.BlockSpec(memory_space=pltpu.VMEM)
    dma = pltpu.SemaphoreType.DMA
    pair = jax.ShapeDtypeStruct((2, TOK, D), BF)

    def held(*shape, kind=BF):
        return pltpu.VMEM(shape, kind)

    def block_of():
        return held(GROUP, 16, WIDE)

    return pl.pallas_call(
        span_kernel,
        name="span",
        out_shape=(
            pair, pair, jax.ShapeDtypeStruct((2, D, HALF), BF), jax.ShapeDtypeStruct((2, HALF, D), BF)
        ),
        in_specs=[anywhere] * 3 + [inside] * 2 + [anywhere] * 2 + [inside],
        out_specs=(anywhere,) * 4,
        scratch_shapes=[
            held(TOK, D), held(TOK, D), held(4, TOK, D), held(3, 1, TOK, kind=jnp.int32),
            held(TOK, WIDE), held(TOK, WIDE), held(TOK, WIDE), *[block_of() for _ in range(7)],
            held(2, TOK, D), held(2, TOK, D), held(D, HID), held(HID, D),
            held(D, HALF), held(D, HALF), held(HALF, D), held(HALF, D),
            held(TOK, W, kind=jnp.float32), held(2, 3 + PARTS, TOK, TOK), held(2, 3 + PARTS, TOK, LINES),
            held(3, TAIL, D), held(TAIL, D),
            held(ROWS, HID, kind=jnp.float32), held(ROWS, HID, kind=jnp.float32),
            held(ROWS, HID), held(ROWS, HID), held(ROWS, HID), held(5, ROWS, 1, kind=jnp.float32),
            dma((5, PARTS)), dma((5, PARTS)), dma((3,)), dma((3,)), dma((3,)), dma((3,)),
            dma((2,)), dma((2, PARTS + 1)), dma((2, 2, PARTS)), dma((2, 2, PARTS)),
            dma((2,)), dma((2,)), dma((2, PARTS)), dma((2, PARTS)), dma((5,)),
        ],
        compiler_params=pltpu.CompilerParams(collective_id=1, has_side_effects=True, vmem_limit_bytes=67043328),
    )(*operands)


def add_pair(pair):
    return (pair[0].astype(jnp.float32) + pair[1].astype(jnp.float32)).astype(BF)[None]


def body(a_input, a_route, b_saved, b_grad, b_route, up_weight, down_weight, router):
    group = lax.axis_size("expert") // EXPERTS
    mine = lax.axis_index("expert") // group
    column = lax.dynamic_slice(router[0], (0, mine), (D, 1)).reshape(1, D).astype(jnp.float32)
    out_a, out_b, up_grad, down_grad = span(
        a_input[0], b_saved[0], b_grad[0], a_route.reshape(1, TOK), b_route.reshape(1, TOK),
        up_weight[0], down_weight[0], column,
    )
    return add_pair(out_a), add_pair(out_b), add_pair(up_grad), add_pair(down_grad)


def solution(mesh):
    rows = P("pipe", "expert", None)
    return jax.shard_map(
        body,
        mesh=mesh,
        in_specs=(rows, rows, rows, rows, rows, P("pipe", None, "expert"), rows, P("pipe", None, None)),
        out_specs=(rows, rows, P("pipe", None, "expert"), rows),
        check_vma=False,
    )
```

```python
import jax
import jax.numpy as jnp
from jax import lax
from jax.experimental import pallas as pl
from jax.experimental.pallas import tpu as pltpu
from jax.sharding import PartitionSpec as P

EPS = 1e-06
MESH = pl.DeviceIdType.MESH
TOK = 128
D = 3584
CAP = 18
EXPERTS = 8
SIDE = 4
GROUP = 8
PARTS = 4
W = D // PARTS
WIDE = 9 * W
HALF = 256
HID = 2 * HALF
LINES = GROUP * 16
TAIL = GROUP * 4
ROWS = 2 * LINES + TAIL
BF = jnp.bfloat16
NEAR = sorted(
    [(i, j) for i in range(SIDE) for j in range(2) if i or j], key=lambda s: min(s[0], SIDE - s[0]) + s[1]
)


class Place:
    def __init__(self):
        self.pipe = lax.axis_index("pipe")
        self.expert = lax.axis_index("expert")
        self.half = lax.rem(self.expert, 2)
        self.x = self.expert // 8
        self.y = lax.rem(self.expert // 2, SIDE)
        self.across = self.expert + 1 - 2 * self.half
        self.mine = self.expert // 4
        self.twin = (self.pipe, self.expert + 2 - 4 * lax.rem(self.y, 2))

    def peer(self, dx, flip):
        x = lax.rem(self.x + dx, SIDE)
        y = 3 - self.y if flip else self.y
        return x, x * 2 + y // 2, (self.pipe, x * 8 + y * 2 + self.half)


def remote(src, dst, send, recv, device):
    return pltpu.make_async_remote_copy(
        src_ref=src, dst_ref=dst, send_sem=send, recv_sem=recv, device_id=device, device_id_type=MESH
    )


def cols(at, width=W):
    return pl.ds(pl.multiple_of(at * W, 128), width)


def part_rows(q):
    return pl.ds(pl.multiple_of(q * W, 128), W)


def rows16(e):
    return pl.ds(pl.multiple_of(e * 16, 16), 16)


def selector(kind, code, part=0):
    row = lax.broadcasted_iota(jnp.int32, (TOK, TOK), 0)
    return ((row == code // 32 * 16 + place(kind, code % 32, part)) & allowed(kind, code % 32)).astype(jnp.float32).astype(BF)


def place(kind, slot, part):
    return {"own0": slot, "own1": slot - 16, "far1": slot + 2, "left": slot - 14 + 4 * part}[kind]


def allowed(kind, slot):
    return {"own0": slot < 16, "own1": slot >= 16, "far1": slot < 14, "left": slot >= 14}[kind]


def unselector(kind, code, part=0):
    lane = lax.broadcasted_iota(jnp.int32, (TOK, LINES), 1)
    slot = code % 32
    hit = (lane // 16 == code // 32) & (lane % 16 == place(kind, slot, part)) & allowed(kind, slot)
    return hit.astype(jnp.float32).astype(BF)


def fill_selectors(make, sel, t, own_code, far_code):
    sel[t, 0] = make("own0", own_code)
    sel[t, 1] = make("own1", own_code)
    sel[t, 2] = make("far1", far_code)
    for q in range(PARTS):
        sel[t, 3 + q] = make("left", far_code, q)


def codes_of(ids):
    i = lax.broadcasted_iota(jnp.int32, (TOK, TOK), 0)
    j = lax.broadcasted_iota(jnp.int32, (TOK, TOK), 1)
    wide = jnp.broadcast_to(ids, (TOK, TOK))
    col = jnp.sum(jnp.where(i == j, wide, 0).astype(jnp.float32), axis=1, keepdims=True).astype(jnp.int32)
    same = col == wide
    slot_row = jnp.sum(jnp.where(same & (i < j), 1.0, 0.0), axis=0, keepdims=True).astype(jnp.int32)
    slot_col = jnp.sum(jnp.where(same & (j < i), 1.0, 0.0), axis=1, keepdims=True).astype(jnp.int32)
    return ids * 32 + slot_row, col * 32 + slot_col


def dot(a, b):
    return jnp.dot(a, b, preferred_element_type=jnp.float32)


def dot_nt(a, b):
    return lax.dot_general(a, b, (((1,), (1,)), ((), ())), preferred_element_type=jnp.float32)


def dot_tn(a, b):
    return lax.dot_general(a, b, (((0,), (0,)), ((), ())), preferred_element_type=jnp.float32)


def gather_tail(q):
    r = lax.broadcasted_iota(jnp.int32, (TAIL, LINES), 0)
    c = lax.broadcasted_iota(jnp.int32, (TAIL, LINES), 1)
    return ((c // 16 == r // 4) & (c % 16 == 4 * q + r % 4)).astype(jnp.float32).astype(BF)


def spread_tail(q):
    c = lax.broadcasted_iota(jnp.int32, (LINES, TAIL), 0)
    r = lax.broadcasted_iota(jnp.int32, (LINES, TAIL), 1)
    return ((c // 16 == r // 4) & (c % 16 == 4 * q + r % 4)).astype(jnp.float32).astype(BF)


def span_kernel(
    ax, bx, bc, a_ids, b_ids, up_in, down_in, column,
    oa, ob, up_out, down_out,
    own_a, far_a, got_b, ids, send_a, send_bx, send_bc, ra, rbx, rbc,
    ret_a, ret_b, ga, gb, own, far, fin, up, down, up_got, up_far, down_got, down_far,
    left, sel, sums, tails, tail_ret, hidden, hidden_a, act_grad, act, act_a, hid_grad, stat, stat_a,
    zsend, zrecv, csend, crecv, psend, precv, gsend, grecv, fsend, frecv, wsend, wrecv, dsend, drecv, out_sem, local,
):
    me = Place()
    across = (me.pipe, me.across)
    mirror = (7 - me.pipe, me.expert)
    mirror_across = (7 - me.pipe, me.across)
    a_to = lax.rem(me.pipe + 1, 8)
    a_from = lax.rem(me.pipe + 7, 8)
    b_to = lax.rem(8 - me.pipe, 8)
    stays = b_to == me.pipe
    barrier = pltpu.get_barrier_semaphore()
    greet = [me.peer(i, j)[2] for i, j in NEAR] + [me.twin, across, mirror, mirror_across]
    greet += [(a_to, me.expert), (a_to, me.across), (a_from, me.expert), (a_from, me.across), (b_to, me.across)]
    for device in greet:
        pl.semaphore_signal(barrier, inc=1, device_id=device, device_id_type=MESH)

    @pl.when(jnp.logical_not(stays))
    def _():
        pl.semaphore_signal(barrier, inc=1, device_id=(b_to, me.expert), device_id_type=MESH)

    loads = [
        pltpu.make_async_copy(ax, own_a, local.at[0]),
        pltpu.make_async_copy(up_in, up.at[:, pl.ds(0, HALF)], local.at[1]),
        pltpu.make_async_copy(down_in, down.at[pl.ds(0, HALF)], local.at[2]),
    ]
    for copy in loads:
        copy.start()
    pl.semaphore_wait(barrier, len(greet) + 1 - stays.astype(jnp.int32))

    small = [
        remote(src, ids.at[i], csend.at[i], crecv.at[i], to)
        for i, (src, to) in enumerate(((a_ids, across), (b_ids, mirror), (b_ids, mirror_across)))
    ]
    weights = [
        remote(up_in, up.at[:, pl.ds(HALF, HALF)], wsend.at[0], wrecv.at[0], me.twin),
        remote(down_in, down.at[pl.ds(HALF, HALF)], wsend.at[1], wrecv.at[1], me.twin),
    ]
    for copy in small + weights:
        copy.start()

    def z_copy(lane, q):
        src, dst, to = [
            (ax, far_a, across),
            (bx, got_b.at[0], mirror),
            (bx, got_b.at[1], mirror_across),
            (bc, got_b.at[2], mirror),
            (bc, got_b.at[3], mirror_across),
        ][lane]
        return remote(src.at[:, cols(q)], dst.at[:, cols(q)], zsend.at[lane, q], zrecv.at[lane, q], to)

    for lanes in ((1, 2), (3, 4), (0,)):
        @pl.loop(0, PARTS)
        def _(q):
            for lane in lanes:
                z_copy(lane, q).start()

    def spread(t, send, recv, at, early=False):
        sem = precv.at[3 if early else t]
        pltpu.make_async_copy(send.at[rows16(me.mine), cols(at)], recv.at[me.x * 2, :, cols(at)], sem).start()
        for i, j in NEAR:
            x, e, device = me.peer(i, j)
            remote(
                send.at[rows16(e), cols(at)], recv.at[me.x * 2 + j, :, cols(at)], psend.at[t], sem, device
            ).start()

    def spread_back(t, send, recv, at, sem):
        pltpu.make_async_copy(
            send.at[me.x * 2, :, cols(at)], recv.at[me.mine, :, cols(at)], grecv.at[t, sem]
        ).start()
        for i, j in NEAR:
            x, e, device = me.peer(i, j)
            remote(
                send.at[x * 2 + j, :, cols(at)], recv.at[me.mine, :, cols(at)], gsend.at[t], grecv.at[t, sem], device
            ).start()

    def arrived(ref, sem):
        pltpu.make_async_copy(ref, ref, sem).wait()

    def block(ref, at):
        return ref[:, :, cols(at)].reshape(LINES, W)

    def put(ref, at, value):
        ref[:, :, cols(at)] = value.reshape(GROUP, 16, W)

    recvs = (ra, rbx, rbc)
    sets = ((0, LINES), (LINES, LINES), (2 * LINES, TAIL))

    def rows_of(t, s, q):
        return block(recvs[t], PARTS * s + q) if s < 2 else tails[t, :, cols(q)]

    def put_rows(t, s, q, value):
        if s < 2:
            put(recvs[t], PARTS * s + q, value)
        else:
            tails[t, :, cols(q)] = value

    def pick_tail(t):
        @pl.loop(0, PARTS)
        def _(q):
            tails[t, :, cols(q)] = dot(gather_tail(q), block(recvs[t], 2 * PARTS)).astype(BF)

    def put_tail(ret):
        left_ret = dot(spread_tail(0), tail_ret[:, cols(0)])
        for q in range(1, PARTS):
            left_ret += dot(spread_tail(q), tail_ret[:, cols(q)])
        put(ret, 2 * PARTS, left_ret.astype(BF))

    def norm_rows(t, s):
        at, n = sets[s]
        rows = pl.ds(at, n)
        hid, st = (hidden, stat) if t else (hidden_a, stat_a)
        st[0, rows] = jnp.zeros((n, 1), jnp.float32)
        st[1, rows] = jnp.zeros((n, 1), jnp.float32)
        hid[rows] = jnp.zeros((n, HID), jnp.float32)

        @pl.loop(0, PARTS)
        def _(q):
            x = rows_of(t, s, q).astype(jnp.float32)
            st[0, rows] += jnp.sum(x * x, axis=1, keepdims=True)

        st[0, rows] = lax.rsqrt(st[0, rows] / D + EPS)

        @pl.loop(0, PARTS)
        def _(q):
            normed = (rows_of(t, s, q).astype(jnp.float32) * st[0, rows]).astype(BF)
            put_rows(t, s, q, normed)
            hid[rows] += dot(normed, up[part_rows(q)])
            st[1, rows] += jnp.sum(normed.astype(jnp.float32) * column[0:1, cols(q)], axis=1, keepdims=True)

        st[2, rows] = jax.nn.sigmoid(st[1, rows])

    def forward_rows(s):
        at, n = sets[s]
        rows = pl.ds(at, n)
        norm_rows(0, s)
        h = hidden_a[rows]
        act_a[rows] = (h * jax.nn.sigmoid(h)).astype(BF)

    def out_rows(s, q):
        at, n = sets[s]
        rows = pl.ds(at, n)
        value = (stat_a[2, rows] * dot(act_a[rows], down[:, cols(q)])).astype(BF)
        if s < 2:
            put(ret_a, PARTS * s + q, value)
        else:
            tail_ret[:, cols(q)] = value

    def gate_rows(s):
        at, n = sets[s]
        rows = pl.ds(at, n)
        act_grad[rows] = jnp.zeros((n, HID), jnp.float32)

        @pl.loop(0, PARTS)
        def _(q):
            cot = (rows_of(2, s, q).astype(jnp.float32) * stat[2, rows]).astype(BF)
            put_rows(2, s, q, cot)
            act_grad[rows] += dot_nt(cot, down[:, cols(q)])

        h, g = hidden[rows], act_grad[rows]
        sig = jax.nn.sigmoid(h)
        a = (h * sig).astype(BF)
        act[rows] = a
        hg = (g * sig * (1.0 + h * (1.0 - sig))).astype(BF)
        hid_grad[rows] = hg
        score_part = jnp.sum(a.astype(jnp.float32) * g, axis=1, keepdims=True) * (1.0 - stat[2, rows])
        stat[3, rows] = score_part
        along = jnp.sum(hg.astype(jnp.float32) * h, axis=1, keepdims=True) + score_part * stat[1, rows]
        stat[4, rows] = along / D

    def back_rows(s, q):
        at, n = sets[s]
        rows = pl.ds(at, n)
        grad = dot_nt(hid_grad[rows], up[part_rows(q)]) + stat[3, rows] * column[0:1, cols(q)]
        value = stat[0, rows] * (grad - rows_of(1, s, q).astype(jnp.float32) * stat[4, rows])
        if s < 2:
            put(ret_b, PARTS * s + q, value.astype(BF))
        else:
            tail_ret[:, cols(q)] = value.astype(BF)

    def far_copy(t, to, q):
        return remote(
            far.at[t, :, cols(q)], fin.at[t, 1, :, cols(q)], fsend.at[t, 1, q], frecv.at[t, 1, q], (to, me.across)
        )

    def own_copy(t, to, q):
        return remote(
            own.at[t, :, cols(q)], fin.at[t, 0, :, cols(q)], fsend.at[t, 0, q], frecv.at[t, 0, q], (to, me.expert)
        )

    def own_stay(t, q):
        return pltpu.make_async_copy(own.at[t, :, cols(q)], fin.at[t, 0, :, cols(q)], frecv.at[t, 0, q])

    def out_copy(t, out, q):
        return pltpu.make_async_copy(fin.at[t, 0, :, cols(q)], out.at[:, cols(q)], out_sem.at[t, q])

    ends = ((ga, own_a, oa, a_to), (gb, got_b.at[2], ob, b_to))

    def collect_edge(t):
        arrived(ends[t][0].at[:, :, pl.ds(2 * D, W)], grecv.at[t, PARTS])

    def collect(t, q):
        recv, base, out, to = ends[t]
        arrived(recv.at[:, :, pl.ds(0, 2 * W)], grecv.at[t, q])
        second = block(recv, PARTS + q)
        far[t, :, cols(q)] = (dot(sums[t, 2], second) + dot(sums[t, 3 + q], block(recv, 2 * PARTS))).astype(BF)
        far_copy(t, to, q).start()
        own[t, :, cols(q)] = (
            base[:, cols(q)].astype(jnp.float32) + dot(sums[t, 0], block(recv, q)) + dot(sums[t, 1], second)
        ).astype(BF)
        if t == 0:
            own_copy(t, to, q).start()
        else:
            @pl.when(stays)
            def _():
                own_stay(t, q).start()

            @pl.when(jnp.logical_not(stays))
            def _():
                own_copy(t, to, q).start()

    def down_part(at, q):
        total = 0.0
        for s, (first, n) in enumerate(sets):
            total += dot_tn(act[pl.ds(first, n), pl.ds(at, HALF)], rows_of(2, s, q))
        return total

    def up_part(at, q):
        total = 0.0
        for s, (first, n) in enumerate(sets):
            total += dot_tn(rows_of(1, s, q), hid_grad[pl.ds(first, n), pl.ds(at, HALF)])
        return total

    def grad_copies(q):
        return [
            remote(down_far.at[:, cols(q)], down_got.at[:, cols(q)], dsend.at[0, q], drecv.at[0, q], me.twin),
            remote(up_far.at[part_rows(q)], up_got.at[part_rows(q)], dsend.at[1, q], drecv.at[1, q], me.twin),
        ]

    a_row, a_col = codes_of(a_ids[...])
    sel[0, 0] = selector("own0", a_row)
    loads[0].wait()

    @pl.loop(0, PARTS)
    def _(q):
        send_a[:, cols(q)] = dot(sel[0, 0], own_a[:, cols(q)]).astype(BF)
        spread(0, send_a, ra, q, early=True)

    for copy in small:
        copy.wait()
    b_row, b_col = codes_of(ids[1])
    b_far_row, b_far_col = codes_of(ids[2])
    fill_selectors(selector, sel, 1, b_row, b_far_row)

    def slot_part(t, send, recv, q):
        z_copy(2 * t - 1, q).wait()
        here = got_b[2 * t - 2, :, cols(q)]
        send[:, cols(q)] = dot(sel[1, 0], here).astype(BF)
        spread(t, send, recv, q)
        z_copy(2 * t, q).wait()
        there = got_b[2 * t - 1, :, cols(q)]
        send[:, cols(PARTS + q)] = (dot(sel[1, 1], here) + dot(sel[1, 2], there)).astype(BF)
        left[...] += dot(sel[1, 3 + q], there)
        spread(t, send, recv, PARTS + q)

    def slot_tail(t, send, recv):
        send[:, 2 * D:] = left[...].astype(BF)
        spread(t, send, recv, 2 * PARTS)
        left[...] = jnp.zeros_like(left)

    left[...] = jnp.zeros_like(left)

    @pl.loop(0, PARTS)
    def _(q):
        slot_part(1, send_bx, rbx, q)

    slot_tail(1, send_bx, rbx)
    a_far_row, a_far_col = codes_of(ids[0])
    fill_selectors(selector, sel, 0, a_row, a_far_row)
    fill_selectors(unselector, sums, 0, a_col, a_far_col)
    fill_selectors(unselector, sums, 1, b_col, b_far_col)

    for q in range(PARTS):
        slot_part(2, send_bc, rbc, q)
        if q == 1:
            loads[1].wait()
            weights[0].wait()
            arrived(rbx, precv.at[1])
            pick_tail(1)
            for s in (2, 0, 1):
                norm_rows(1, s)
        if q == 2:
            arrived(ra.at[:, :, pl.ds(0, D)], precv.at[3])
            forward_rows(0)
    slot_tail(2, send_bc, rbc)

    loads[2].wait()
    weights[1].wait()
    arrived(rbc, precv.at[2])
    pick_tail(2)
    for s in (2, 0, 1):
        gate_rows(s)
        if s == 2:
            @pl.loop(0, PARTS)
            def _(q):
                back_rows(2, q)

            put_tail(ret_b)
            spread_back(1, ret_b, gb, 2 * PARTS, PARTS)

    @pl.loop(0, PARTS)
    def _(q):
        back_rows(1, q)
        spread_back(1, ret_b, gb, PARTS + q, q)
        back_rows(0, q)
        spread_back(1, ret_b, gb, q, q)

    @pl.loop(0, PARTS)
    def _(q):
        down_far[:, cols(q)] = down_part(HALF, q).astype(BF)
        up_far[part_rows(q)] = up_part(HALF, q).astype(BF)
        for copy in grad_copies(q):
            copy.start()

    @pl.loop(0, PARTS)
    def _(q):
        out_rows(0, q)
        spread_back(0, ret_a, ga, q, q)

    @pl.loop(0, PARTS)
    def _(q):
        z_copy(0, q).wait()
        there = far_a[:, cols(q)]
        send_a[:, cols(PARTS + q)] = (dot(sel[0, 1], own_a[:, cols(q)]) + dot(sel[0, 2], there)).astype(BF)
        left[...] += dot(sel[0, 3 + q], there)
        spread(0, send_a, ra, PARTS + q)

    send_a[:, 2 * D:] = left[...].astype(BF)
    spread(0, send_a, ra, 2 * PARTS)

    collect_edge(1)

    @pl.loop(0, PARTS)
    def _(q):
        collect(1, q)

    arrived(ra.at[:, :, pl.ds(D, D + W)], precv.at[0])
    pick_tail(0)
    forward_rows(2)

    @pl.loop(0, PARTS)
    def _(q):
        out_rows(2, q)

    put_tail(ret_a)
    spread_back(0, ret_a, ga, 2 * PARTS, PARTS)
    forward_rows(1)

    @pl.loop(0, PARTS)
    def _(q):
        out_rows(1, q)
        spread_back(0, ret_a, ga, PARTS + q, q)

    collect_edge(0)

    @pl.loop(0, PARTS)
    def _(q):
        collect(0, q)

    @pl.loop(0, PARTS)
    def _(q):
        for copy in grad_copies(q):
            copy.wait()
        down_got[:, cols(q)] = (down_got[:, cols(q)].astype(jnp.float32) + down_part(0, q)).astype(BF)
        up_got[part_rows(q)] = (up_got[part_rows(q)].astype(jnp.float32) + up_part(0, q)).astype(BF)

    stores = [
        pltpu.make_async_copy(up_got, up_out, local.at[3]),
        pltpu.make_async_copy(down_got, down_out, local.at[4]),
    ]
    for copy in stores:
        copy.start()

    for t in (1, 0):
        recv, base, out, to = ends[t]

        @pl.loop(0, PARTS)
        def _(q):
            if t == 0:
                own_copy(t, to, q).wait()
            else:
                @pl.when(jnp.logical_not(stays))
                def _():
                    own_copy(t, to, q).wait()

                @pl.when(stays)
                def _():
                    own_stay(t, q).wait()
            far_copy(t, to, q).wait()
            fin[t, 0, :, cols(q)] = (
                fin[t, 0, :, cols(q)].astype(jnp.float32) + fin[t, 1, :, cols(q)].astype(jnp.float32)
            ).astype(BF)
            out_copy(t, out, q).start()

    for t, recv in enumerate(recvs):
        most = recv.at[pl.ds(0, GROUP - 1)]
        remote(most, most, psend.at[t], precv.at[t], across).wait_send()
    for t, (recv, base, out, to) in enumerate(ends):
        most = recv.at[pl.ds(0, GROUP - 1)]
        remote(most, most, gsend.at[t], grecv.at[t, 0], across).wait_send()

        @pl.loop(0, PARTS)
        def _(q):
            out_copy(t, out, q).wait()
    for copy in stores:
        copy.wait()


def span(*operands):
    anywhere = pl.BlockSpec(memory_space=pl.ANY)
    inside = pl.BlockSpec(memory_space=pltpu.VMEM)
    dma = pltpu.SemaphoreType.DMA
    rows = jax.ShapeDtypeStruct((TOK, D), BF)

    def held(*shape, kind=BF):
        return pltpu.VMEM(shape, kind)

    def block_of():
        return held(GROUP, 16, WIDE)

    return pl.pallas_call(
        span_kernel,
        name="span",
        out_shape=(
            rows, rows, jax.ShapeDtypeStruct((D, HALF), BF), jax.ShapeDtypeStruct((HALF, D), BF)
        ),
        in_specs=[anywhere] * 3 + [inside] * 2 + [anywhere] * 2 + [inside],
        out_specs=(anywhere,) * 4,
        scratch_shapes=[
            held(TOK, D), held(TOK, D), held(4, TOK, D), held(3, 1, TOK, kind=jnp.int32),
            held(TOK, WIDE), held(TOK, WIDE), held(TOK, WIDE), *[block_of() for _ in range(7)],
            held(2, TOK, D), held(2, TOK, D), held(2, 2, TOK, D), held(D, HID), held(HID, D),
            held(D, HALF), held(D, HALF), held(HALF, D), held(HALF, D),
            held(TOK, W, kind=jnp.float32), held(2, 3 + PARTS, TOK, TOK), held(2, 3 + PARTS, TOK, LINES),
            held(3, TAIL, D), held(TAIL, D),
            *[held(ROWS, HID, kind=jnp.float32) for _ in range(3)],
            held(ROWS, HID), held(ROWS, HID), held(ROWS, HID),
            held(5, ROWS, 1, kind=jnp.float32), held(3, ROWS, 1, kind=jnp.float32),
            dma((5, PARTS)), dma((5, PARTS)), dma((3,)), dma((3,)), dma((3,)), dma((4,)),
            dma((2,)), dma((2, PARTS + 1)), dma((2, 2, PARTS)), dma((2, 2, PARTS)),
            dma((2,)), dma((2,)), dma((2, PARTS)), dma((2, PARTS)), dma((2, PARTS)), dma((5,)),
        ],
        compiler_params=pltpu.CompilerParams(collective_id=1, has_side_effects=True, vmem_limit_bytes=67043328),
    )(*operands)


def body(a_input, a_route, b_saved, b_grad, b_route, up_weight, down_weight, router):
    group = lax.axis_size("expert") // EXPERTS
    mine = lax.axis_index("expert") // group
    column = lax.dynamic_slice(router[0], (0, mine), (D, 1)).reshape(1, D).astype(jnp.float32)
    out_a, out_b, up_grad, down_grad = span(
        a_input[0], b_saved[0], b_grad[0], a_route.reshape(1, TOK), b_route.reshape(1, TOK),
        up_weight[0], down_weight[0], column,
    )
    return out_a[None], out_b[None], up_grad[None], down_grad[None]


def solution(mesh):
    rows = P("pipe", "expert", None)
    return jax.shard_map(
        body,
        mesh=mesh,
        in_specs=(rows, rows, rows, rows, rows, P("pipe", None, "expert"), rows, P("pipe", None, None)),
        out_specs=(rows, rows, P("pipe", None, "expert"), rows),
        check_vma=False,
    )
```
